32 devices in a mesh: groups: 2 (over y), tensor: 4 (over z), store: 4 (over x, core).
Axes of the slice: x: 2, y: 2, z: 4, core: 2. Of those that a mesh axis runs over, the one named last changes fastest.
Arguments:
- tokens: bfloat16 [4096, 8192], P(('groups', 'store', 'tensor')), parts along dimension 0, may hold values from -32 to 32
- query_weight: bfloat16 [8192, 8192], P(None, 'tensor'), may hold values from -0.0625 to 0.0625
- key_value_weight: bfloat16 [8192, 2048], P(None, 'tensor'), may hold values from -0.0625 to 0.0625
- adapter_down_maps: bfloat16 [32, 128, 8192], P('store', None, 'tensor'), may hold values from -0.0625 to 0.0625
- adapter_up_query: bfloat16 [32, 64, 8192], P('store', None, 'tensor'), may hold values from -0.375 to 0.375
- adapter_up_key_value: bfloat16 [32, 64, 2048], P('store', None, 'tensor'), may hold values from -0.375 to 0.375
- adapter_row_table: int32 [64], P('groups'), parts along dimension 0, may hold values from 0 to 31, as said below
- request_adapter_ids: int32 [8, 4], P('groups'), parts along dimension 0, may hold values from 0 to 31, as said below
- token_request_ids: int32 [8, 512], P(('groups', 'store')), parts along dimension 0, may hold values from 0 to 3, never falling along the last dimension, each value on 1 to 256 neighbouring positions
Outputs:
- attention: bfloat16 [4096, 8192], P(('groups', 'store'), 'tensor'), parts along dimension 0
The draws below stay inside these ranges and needn't reach their ends.
There are 2 independent parts, one for each index of `groups`. The reference program is written for one: setup_inputs(seed, part) draws one part's arguments, and reference() takes and returns one part's arrays. A program takes and returns all parts, laid end to end along the dimension named above; an argument that names none is the same for every part. Nothing has to cross between parts.
Inputs may be any that keep to these rules, and one draw needn't show every extreme that they name: A permutation: adapter a lies in row adapter_row_table[a] of the adapter arrays, on store index adapter_row_table[a] // 8. `request_adapter_ids`: the 4 requests of one store batch use adapters held on 4 different store indices. `token_request_ids`: requests are contiguous runs of a store batch, each of 1 to 256 tokens.
All inputs are finite; a program needn't handle non-finite values.
Results may differ from the reference program's by a relative error of at most 0.012.
The reference program's roundings to bfloat16 on the way (of `low`, `query`, `keys`, `values` and `weights`) count: a program that leaves them out, or rounds other values in their place, can miss the bound.
Values may be sent and summed in bfloat16 or wider, within the bound.
A program may use at most 128 MiB of HBM per device.

```python
import math
import jax
import jax.numpy as jnp
import numpy as np
from jax import lax

MODEL_WIDTH = 8192
QUERY_HEADS = 64
KEY_VALUE_HEADS = 8
HEAD_SIZE = 128
ADAPTER_RANK = 64
STORE_REQUESTS = 4
TOK_ST = 512
SLOTS = 8
TOKENS = 2048
ADAPTER_COUNT = 32
N_TENSOR = 4
N_STORE = 4


def draw_tokens(key, part):
    values = jnp.clip(jax.random.normal(jax.random.fold_in(key, 3), (TOKENS, MODEL_WIDTH), jnp.float32), -4.0, 4.0)
    return values.astype(jnp.bfloat16)


def place_slot(owners, locals_table, row_pick, col_pick, slot_value):
    target = slot_value // SLOTS
    row_index = jnp.arange(N_STORE, dtype=jnp.int32)[:, None]
    col_index = jnp.arange(N_STORE, dtype=jnp.int32)[None, :]
    in_row = row_index == row_pick
    current = owners[row_pick, col_pick]
    moved = jnp.where(in_row & (owners == target), current, owners)
    moved = jnp.where(in_row & (col_index == col_pick), target, moved)
    locals_new = jnp.where(in_row & (col_index == col_pick), slot_value % SLOTS, locals_table)
    return (moved, locals_new)


def owner_rows(row_key):
    return jax.random.permutation(row_key, N_STORE).astype(jnp.int32)


def placement_tables(key):
    adapter_total = SLOTS * N_STORE
    order = jax.random.permutation(jax.random.fold_in(key, 21), adapter_total).astype(jnp.int32)
    inverse = jnp.zeros((adapter_total,), jnp.int32).at[order].set(jnp.arange(adapter_total, dtype=jnp.int32))
    row_keys = jax.random.split(jax.random.fold_in(key, 22), N_STORE)
    owners = jax.vmap(owner_rows)(row_keys)
    locals_table = jax.random.randint(jax.random.fold_in(key, 23), (N_STORE, N_STORE), 0, SLOTS).astype(jnp.int32)
    first_row = jax.random.randint(jax.random.fold_in(key, 24), (), 0, N_STORE).astype(jnp.int32)
    second_row = ((first_row + 1 + jax.random.randint(jax.random.fold_in(key, 25), (), 0, N_STORE - 1)) % N_STORE).astype(jnp.int32)
    first_col = jax.random.randint(jax.random.fold_in(key, 26), (), 0, STORE_REQUESTS).astype(jnp.int32)
    second_col = jax.random.randint(jax.random.fold_in(key, 27), (), 0, STORE_REQUESTS).astype(jnp.int32)
    owners, locals_table = place_slot(owners, locals_table, first_row, first_col, order[adapter_total - 1])
    owners, locals_table = place_slot(owners, locals_table, second_row, second_col, order[0])
    positions_list = owners[:, :STORE_REQUESTS] * SLOTS + locals_table[:, :STORE_REQUESTS]
    return (order, inverse[positions_list].astype(jnp.int32))


def draw_adapter_row_table(key, part):
    return placement_tables(key)[0]


def draw_request_adapter_ids(key, part):
    return placement_tables(key)[1]


def steps_of(own_key, shape, shards, smallest, top_value):
    def one(axis_at, shards_of):
        draws = jax.random.uniform(jax.random.fold_in(jax.random.fold_in(own_key, 6), axis_at), (shards_of,), jnp.float32, smallest / len(shards), top_value / len(shards))
        return jnp.repeat(jnp.exp(draws), shape[axis_at] // shards_of).reshape((-1,) + (1,) * (len(shape) - axis_at - 1))

    loudness = one(*shards[0])
    for cut in shards[1:]:
        loudness = loudness * one(*cut)
    return loudness


def length_profile(count, total, limit, skew):
    weights = [(1 << 20) // math.isqrt(standing ** skew) + 1 for standing in range(2, count + 1)]
    surplus, holding = total - limit - (count - 1), [1] * (count - 1)
    while surplus > 0:
        candidates = [i for i in range(count - 1) if holding[i] < limit]
        mass, remaining = sum([weights[i] for i in candidates]), surplus
        for i in candidates:
            extra = min(limit - holding[i], max(1, remaining * weights[i] // mass), surplus)
            holding[i] = holding[i] + extra
            surplus = surplus - extra
    return np.array([limit] + holding)


def uneven_parts(rng, amount, total, bound, skew):
    if amount == 2:
        one = jax.random.randint(rng, (), max(1, total - bound), min(bound, total - 1) + 1)
        return jnp.stack([one, total - one])
    tallies = jnp.asarray(length_profile(amount, total, bound, skew), jnp.int32)
    couples = (amount - 1) // 2
    giver, taker = tallies[1:1 + 2 * couples:2], tallies[2:2 + 2 * couples:2]
    slack = jnp.minimum(giver - 1, bound - taker)
    passed = jax.random.randint(jax.random.fold_in(rng, 1), (couples,), 0, 1 << 20) % (slack + 1)
    tallies = tallies.at[1:1 + 2 * couples:2].set(giver - passed).at[2:2 + 2 * couples:2].set(taker + passed)
    return tallies[jax.random.permutation(jax.random.fold_in(rng, 2), amount)]


def noise(rng, shape, scale, bound, pieces=(), held_as=jnp.bfloat16):
    values = scale * jax.random.normal(rng, shape, jnp.float32)
    if pieces:
        values = values * steps_of(rng, shape, pieces, -0.22, 0.18)
    return jnp.clip(values, -bound, bound).astype(held_as)


def setup_inputs(seed: int = 0, part: int = 0) -> dict:
    seeds = jax.random.split(jax.random.key(seed), 10)
    part_splits = jax.random.split(jax.random.fold_in(seeds[9], part), 10)
    return {
        "tokens": draw_tokens(jax.random.fold_in(jax.random.fold_in(seeds[9], part), 71), part),
        "query_weight": noise(seeds[1], (MODEL_WIDTH, QUERY_HEADS * HEAD_SIZE), MODEL_WIDTH ** -0.5, 0.0625, ((1, 4),)),
        "key_value_weight": noise(seeds[2], (MODEL_WIDTH, 2 * KEY_VALUE_HEADS * HEAD_SIZE), MODEL_WIDTH ** -0.5, 0.0625, ((1, 4),)),
        "adapter_down_maps": noise(seeds[3], (ADAPTER_COUNT, 2 * ADAPTER_RANK, MODEL_WIDTH), MODEL_WIDTH ** -0.5, 0.0625, ((0, 4), (2, 4))),
        "adapter_up_query": noise(seeds[4], (ADAPTER_COUNT, ADAPTER_RANK, QUERY_HEADS * HEAD_SIZE), (4 * ADAPTER_RANK) ** -0.5, 0.375, ((0, 4), (2, 4))),
        "adapter_up_key_value": noise(seeds[5], (ADAPTER_COUNT, ADAPTER_RANK, 2 * KEY_VALUE_HEADS * HEAD_SIZE), (4 * ADAPTER_RANK) ** -0.5, 0.375, ((0, 4), (2, 4))),
        "adapter_row_table": draw_adapter_row_table(jax.random.fold_in(jax.random.fold_in(seeds[9], part), 71), part),
        "request_adapter_ids": draw_request_adapter_ids(jax.random.fold_in(jax.random.fold_in(seeds[9], part), 71), part),
        "token_request_ids": jax.vmap(lambda own: jnp.searchsorted(jnp.cumsum(uneven_parts(own, STORE_REQUESTS, TOK_ST, TOK_ST // 2, 2)), jnp.arange(TOK_ST), side="right"))(jax.random.split(part_splits[8], N_STORE)).reshape((N_STORE, TOK_ST)).astype(jnp.int32),
    }


adapter_scale = 2.0
rope_theta = 500000.0

def token_positions(segment_row):
    members = segment_row[:, None] == jnp.arange(STORE_REQUESTS, dtype=jnp.int32)[None, :]
    counts = lax.optimization_barrier(jnp.sum(members.astype(jnp.int32), axis=0)).astype(jnp.int32)
    starts = (jnp.cumsum(counts) - counts).astype(jnp.int32)
    first_index = lax.optimization_barrier(jnp.sum(jnp.where(members, starts[None, :], 0), axis=1)).astype(jnp.int32)
    return jnp.arange(segment_row.shape[0], dtype=jnp.int32) - first_index

def rotary(heads_values, positions):
    half_size = heads_values.shape[-1] // 2
    exponent = jnp.arange(half_size, dtype=jnp.float32) * (2.0 / heads_values.shape[-1])
    frequency = jnp.exp(-exponent * math.log(rope_theta))
    angles = positions.astype(jnp.float32)[:, None] * frequency[None, :]
    cosine = jnp.cos(angles)[:, None, :]
    sine = jnp.sin(angles)[:, None, :]
    lower = heads_values[..., :half_size]
    upper = heads_values[..., half_size:]
    return jnp.concatenate([lower * cosine - upper * sine, upper * cosine + lower * sine], axis=-1)

def reference(tokens, query_weight, key_value_weight, adapter_down_maps, adapter_up_query, adapter_up_key_value, adapter_row_table, request_adapter_ids, token_request_ids):
    group_size = QUERY_HEADS // KEY_VALUE_HEADS
    pair_count = N_TENSOR // 2
    pair_heads = 2 * KEY_VALUE_HEADS // N_TENSOR
    slot_table = adapter_row_table[request_adapter_ids].astype(jnp.int32)
    batches = tokens.reshape(N_STORE, TOK_ST, MODEL_WIDTH)

    def one_batch(inputs):
        gathered_rows, positions_list, segment_row = inputs
        members = segment_row[:, None] == jnp.arange(STORE_REQUESTS, dtype=jnp.int32)[None, :]
        member_float = members.astype(jnp.float32)
        member_half = members.astype(jnp.bfloat16)
        down_product = adapter_down_maps[positions_list].astype(jnp.float32)
        projected = jnp.einsum('td,krd->tkr', gathered_rows.astype(jnp.float32), down_product)
        low = lax.optimization_barrier(jnp.sum(projected * member_float[:, :, None], axis=1)).astype(jnp.bfloat16)
        token_query_update = (low[:, None, :ADAPTER_RANK] * member_half[:, :, None]).reshape(TOK_ST, STORE_REQUESTS * ADAPTER_RANK)
        token_key_value_update = (low[:, None, ADAPTER_RANK:] * member_half[:, :, None]).reshape(TOK_ST, STORE_REQUESTS * ADAPTER_RANK)
        query_update = jnp.dot(token_query_update, adapter_up_query[positions_list].reshape(STORE_REQUESTS * ADAPTER_RANK, QUERY_HEADS * HEAD_SIZE), preferred_element_type=jnp.float32)
        key_value_update = jnp.dot(token_key_value_update, adapter_up_key_value[positions_list].reshape(STORE_REQUESTS * ADAPTER_RANK, 2 * KEY_VALUE_HEADS * HEAD_SIZE), preferred_element_type=jnp.float32)
        query_unrotated = jnp.dot(gathered_rows, query_weight, preferred_element_type=jnp.float32) + adapter_scale * query_update
        key_value_unrotated = jnp.dot(gathered_rows, key_value_weight, preferred_element_type=jnp.float32) + adapter_scale * key_value_update
        positions = token_positions(segment_row)
        query = rotary(query_unrotated.reshape(TOK_ST, QUERY_HEADS, HEAD_SIZE), positions).astype(jnp.bfloat16)
        keyval = key_value_unrotated.reshape(TOK_ST, pair_count, 2, pair_heads, HEAD_SIZE)
        keys = rotary(keyval[:, :, 0].reshape(TOK_ST, KEY_VALUE_HEADS, HEAD_SIZE), positions).astype(jnp.bfloat16)
        values = keyval[:, :, 1].reshape(TOK_ST, KEY_VALUE_HEADS, HEAD_SIZE).astype(jnp.bfloat16)
        grouped = query.reshape(TOK_ST, KEY_VALUE_HEADS, group_size, HEAD_SIZE)
        scores = jnp.einsum('tkgd,skd->kgts', grouped.astype(jnp.float32), keys.astype(jnp.float32)) / math.sqrt(HEAD_SIZE)
        token_index = jnp.arange(TOK_ST, dtype=jnp.int32)
        allowed = (segment_row[:, None] == segment_row[None, :]) & (token_index[:, None] >= token_index[None, :])
        scores = jnp.where(allowed, scores, -1e+30)
        scores = scores - lax.optimization_barrier(jnp.max(scores, axis=-1, keepdims=True))
        weights = jnp.exp(scores)
        weights = (weights / lax.optimization_barrier(jnp.sum(weights, axis=-1, keepdims=True))).astype(jnp.bfloat16)
        mixed = jnp.einsum('kgts,skd->tkgd', weights.astype(jnp.float32), values.astype(jnp.float32))
        return mixed.reshape(TOK_ST, QUERY_HEADS * HEAD_SIZE).astype(jnp.bfloat16)
    result = lax.map(one_batch, (batches, slot_table, token_request_ids))
    return result.reshape(TOKENS, QUERY_HEADS * HEAD_SIZE)
```

```python
import functools
import math

import jax
import jax.numpy as jnp
from jax import lax
from jax.experimental import pallas as pl
from jax.experimental.pallas import tpu as pltpu
from jax.sharding import PartitionSpec as P

MODEL_WIDTH = 8192
QUERY_HEADS = 64
KEY_VALUE_HEADS = 8
HEAD_SIZE = 128
ADAPTER_RANK = 64
STORE_REQUESTS = 4
TOK_ST = 512


adapter_scale = 2.0
rope_theta = 500000.0


MAX_RUN = 256
MESH = pl.DeviceIdType.MESH


def project_kernel(
    n,
    stores,
    chunks,
    slots,
    tokens_ref,
    wq_hbm,
    wkv_hbm,
    down_hbm,
    upq_hbm,
    upkv_hbm,
    table_ref,
    request_ref,
    segment_ref,
    out_ref,
    down_picked,
    upq_picked,
    upkv_picked,
    xbuf,
    wq,
    wkv,
    acc_q,
    acc_kv,
    down,
    upq,
    upkv,
    low_part,
    low_own,
    low_got,
    low_all,
    kv_heads,
    kv_got,
    keys_ref,
    values_ref,
    bias_ref,
    cos_ref,
    sin_ref,
    holder_ref,
    token_sem,
    weight_sem,
    recv_sem,
    send_sem,
    adapter_send,
    adapter_recv,
    adapter_own,
    candidate_sem,
    picked_sem,
    part_send,
    part_recv,
    low_send,
    low_recv,
    kv_sem,
    out_sem,
):
    t = lax.axis_index("tensor")
    s = lax.axis_index("store")
    rows = tokens_ref.shape[0]
    width = tokens_ref.shape[1] // chunks
    total = rows * n
    query_width = wq.shape[1]
    keyval_width = wkv.shape[1]
    pair_heads = keyval_width // HEAD_SIZE
    head_local = query_width // HEAD_SIZE
    group_size = QUERY_HEADS // KEY_VALUE_HEADS
    kv_used = max(head_local // group_size, 1)

    def kv_first(rank):
        return rank * head_local // group_size - rank // 2 * pair_heads

    barrier = pltpu.get_barrier_semaphore()
    for d in range(1, n):
        pl.semaphore_signal(
            barrier, inc=1, device_id={"tensor": lax.rem(t + d, n)}, device_id_type=MESH
        )
    for d in range(1, stores):
        pl.semaphore_signal(
            barrier, inc=1, device_id={"store": lax.rem(s + d, stores)}, device_id_type=MESH
        )

    def own_copy(c):
        return pltpu.make_async_copy(
            tokens_ref.at[:, pl.ds(c * width, width)],
            xbuf.at[c, pl.ds(t * rows, rows), :],
            token_sem.at[c],
        )

    def weight_copies(c):
        part = pl.ds(c * width, width)
        return (
            pltpu.make_async_copy(wq_hbm.at[part, :], wq.at[part, :], weight_sem.at[0, c]),
            pltpu.make_async_copy(wkv_hbm.at[part, :], wkv.at[part, :], weight_sem.at[1, c]),
        )

    model_width = wq.shape[0]
    two_ranks = 2 * ADAPTER_RANK
    picked_down = chunks // 2 * width
    picked_up = picked_down + stores * two_ranks
    picked_end = picked_up + stores * ADAPTER_RANK
    candidate_sets = (
        (down_hbm, wq, 0, two_ranks, picked_down, down_picked),
        (upq_hbm, wq, slots * two_ranks, ADAPTER_RANK, picked_up, upq_picked),
        (upkv_hbm, wkv, 0, ADAPTER_RANK, picked_up, upkv_picked),
    )
    candidates = [
        pltpu.make_async_copy(
            source.at[k], held.at[pl.ds(first + k * count, count), :], candidate_sem.at[j, k]
        )
        for j, (source, held, first, count, _, _) in enumerate(candidate_sets)
        for k in range(slots)
    ]
    adapter_pairs = ((down_picked, down), (upq_picked, upq), (upkv_picked, upkv))

    def adapter_block(held, i, at):
        if i == 0:
            return held.at[at]
        return held.at[pl.ds(at * ADAPTER_RANK, ADAPTER_RANK), :]

    own_adapters = [
        pltpu.make_async_copy(source.at[s], adapter_block(held, i, s), adapter_own.at[i])
        for i, (source, held) in enumerate(adapter_pairs)
    ]

    pl.semaphore_wait(barrier, n - 1 + stores - 1)

    def place(side, i):
        return chunks - 1 - i if side == 0 else i

    def stream_copy(side, p, i, own):
        c = place(side, i)
        shard = t - p if side == 0 else t + p
        held = xbuf.at[c, pl.ds(shard * rows, rows), :]
        source = tokens_ref.at[:, pl.ds(c * width, width)] if own else held
        return pltpu.make_async_remote_copy(
            src_ref=source,
            dst_ref=held,
            send_sem=send_sem.at[side, p, i],
            recv_sem=recv_sem.at[side, p, i],
            device_id={"tensor": t + 1 if side == 0 else t - 1},
            device_id_type=MESH,
        )

    def arrival(side, p, i):
        c = place(side, i)
        shard = t - p if side == 0 else t + p
        held = xbuf.at[c, pl.ds(shard * rows, rows), :]
        return pltpu.make_async_remote_copy(
            src_ref=held,
            dst_ref=held,
            send_sem=send_sem.at[side, p - 1, i],
            recv_sem=recv_sem.at[side, p - 1, i],
            device_id={"tensor": t - 1 if side == 0 else t + 1},
            device_id_type=MESH,
        )

    is_end = jnp.logical_or(t == 0, t == n - 1)
    share = chunks // n
    can_send = (t < n - 1, t > 0)
    reach = (t, n - 1 - t)

    def item(shards, j):
        head = share * shards
        rest = chunks - share
        in_head = j < head
        k = jnp.maximum(j - head, 0)
        return (
            jnp.where(in_head, j // share, k // rest) + 1,
            jnp.where(in_head, j % share, share + k % rest),
        )

    def send_item(side, j, own):
        p, i = item(reach[side] + 1, j)
        return stream_copy(side, p - 1, i, own)

    def start_send(side, j):
        p, i = item(reach[side] + 1, j)

        @pl.when(p == 1)
        def _():
            stream_copy(side, 0, i, True).start()

        @pl.when(p > 1)
        def _():
            stream_copy(side, p - 1, i, False).start()

    ahead = 2
    depth = 4
    for j in range(ahead):
        for side in range(2):

            @pl.when(can_send[side])
            def _():
                stream_copy(side, 0, j, True).start()

    for copy in candidates:
        copy.start()
    for c in range(chunks):
        own_copy(c).start()

    tile_q = min(query_width, 512)

    def keyval_unit(c, shard):
        at = pl.ds(pl.multiple_of(shard * rows, rows), rows)
        part = pl.ds(pl.multiple_of(c * width, width), width)
        acc_kv[at, :] += jnp.dot(
            xbuf[c, at, :], wkv[part, :], preferred_element_type=jnp.float32
        )

    def query_unit(c, shard):
        at = pl.ds(pl.multiple_of(shard * rows, rows), rows)
        part = pl.ds(pl.multiple_of(c * width, width), width)

        @pl.loop(0, query_width // tile_q)
        def _(k):
            columns = pl.ds(pl.multiple_of(k * tile_q, tile_q), tile_q)
            acc_q[at, columns] += jnp.dot(
                xbuf[c, at, :], wq[part, columns], preferred_element_type=jnp.float32
            )

    acc_q[...] = jnp.zeros_like(acc_q)
    acc_kv[...] = jnp.zeros_like(acc_kv)
    holds_keys = t % 2 == 0

    def request_column():
        place_row = lax.broadcasted_iota(jnp.int32, (total, total), 0)
        place_column = lax.broadcasted_iota(jnp.int32, (total, total), 1)
        across = segment_ref[...].astype(jnp.float32)
        own = jnp.where(place_row == place_column, across, 0.0)
        return across, jnp.sum(own, axis=1, keepdims=True), place_row >= place_column

    def fill_tables():
        across, down_column, ordered = request_column()
        allowed = jnp.logical_and(down_column == across, ordered)
        bias_ref[...] = jnp.where(allowed, 0.0, -1e30)
        first_index = jnp.sum(jnp.where(across < down_column, 1.0, 0.0), axis=1, keepdims=True)
        place_token = lax.broadcasted_iota(jnp.int32, (total, 1), 0).astype(jnp.float32)
        lane = lax.broadcasted_iota(jnp.int32, (total, HEAD_SIZE), 1)
        exponent = lax.rem(lane, HEAD_SIZE // 2).astype(jnp.float32) * (2.0 / HEAD_SIZE)
        angles = (place_token - first_index) * jnp.exp(-exponent * math.log(rope_theta))
        sine = jnp.sin(angles)
        cos_ref[...] = jnp.cos(angles)
        sin_ref[...] = jnp.where(lane < HEAD_SIZE // 2, -sine, sine)

    def fill_holder():
        _, down_column, _ = request_column()
        holder = jnp.zeros((total, 1), jnp.float32)
        for k in range(STORE_REQUESTS):
            owner = lax.div(table_ref[request_ref[s, k]], slots).astype(jnp.float32)
            holder += jnp.where(down_column == float(k), owner, 0.0)
        holder_ref[...] = holder

    for copy in candidates:
        copy.wait()
    bits = []
    for i in range(stores):
        index = 0
        for k in range(STORE_REQUESTS):
            slot = table_ref[request_ref[i, k]]
            index += jnp.where(lax.div(slot, slots) == s, lax.rem(slot, slots), 0)
        bits.append([lax.rem(lax.div(index, 1 << k), 2) == 1 for k in range(slots.bit_length())])

    def pick(held, first, count, to):
        lanes = min(held.shape[1], 512)

        @pl.loop(0, count // 16)
        def _(r):
            for at in range(0, held.shape[1], lanes):
                columns = slice(at, at + lanes)

                def tile(base, k):
                    return pl.ds(pl.multiple_of(base + k * count + r * 16, 16), 16)

                found = [held[tile(first, k), columns] for k in range(slots)]
                for i in range(stores):
                    left, level = found, 0
                    while len(left) > 1:
                        bit = bits[i][level]
                        left = [
                            jnp.where(bit, left[k + 1], left[k]) if k + 1 < len(left) else left[k]
                            for k in range(0, len(left), 2)
                        ]
                        level += 1
                    held[tile(to, i), columns] = left[0]

    for _, held, first, count, to, _ in candidate_sets:
        pick(held, first, count, to)
    picked_copies = [
        pltpu.make_async_copy(
            held.at[pl.ds(to + i * count, count), :], picked.at[i], picked_sem.at[j, i]
        )
        for j, (_, held, _, count, to, picked) in enumerate(candidate_sets)
        for i in range(stores)
    ]
    for copy in picked_copies:
        copy.start()
    def start_weights(k):
        for c in (k, chunks - 1 - k):
            for copy in weight_copies(c):
                copy.start()

    start_weights(0)
    for copy in picked_copies:
        copy.wait()
    for copy in own_adapters:
        copy.start()
    adapter_sends = []
    for d in range(1, stores):
        for i, (source, held) in enumerate(adapter_pairs):
            peer = lax.rem(s + d, stores)
            copy = pltpu.make_async_remote_copy(
                src_ref=source.at[peer],
                dst_ref=adapter_block(held, i, s),
                send_sem=adapter_send.at[i, d],
                recv_sem=adapter_recv.at[i, d],
                device_id={"store": peer},
                device_id_type=MESH,
            )
            copy.start()
            adapter_sends.append(copy)


    def mask_of(p):
        return jnp.where(holder_ref[...] == float(p), 1.0, 0.0)

    for copy in own_adapters:
        copy.wait()
    for c in range(chunks):
        own_copy(c).wait()

    def low_ready(side):
        first = share * (t if side == 1 else n - 1 - t)
        i = first + share - 1
        shards = reach[side]
        in_rest = share * shards + (shards - 1) * (chunks - share) + i - share
        return jnp.where(shards == 0, 0, jnp.where(i < share, share * shards - 1, in_rest))

    last_step = (n - 1) * chunks - 1
    inner_done = (n - 2) * chunks - 1
    second_at = inner_done + jnp.where(is_end, 1, 0)
    third_at = jnp.where(is_end, last_step - 3, inner_done + 1)
    early_at = jnp.where(is_end, last_step - 2, last_step - 3)
    low_at = jnp.maximum(jnp.maximum(low_ready(0), low_ready(1)), chunks)

    def part_copy(d):
        to = lax.rem(t + d, n)
        return pltpu.make_async_remote_copy(
            src_ref=low_part.at[pl.ds(to * rows, rows), :],
            dst_ref=low_got.at[t],
            send_sem=part_send.at[d],
            recv_sem=part_recv.at[d],
            device_id={"tensor": to},
            device_id_type=MESH,
        )

    def part_arrival(d):
        source = lax.rem(t + n - d, n)
        return pltpu.make_async_remote_copy(
            src_ref=low_got.at[source],
            dst_ref=low_got.at[source],
            send_sem=part_send.at[d],
            recv_sem=part_recv.at[d],
            device_id={"tensor": source},
            device_id_type=MESH,
        )

    def low_copy(d):
        to = lax.rem(t + d, n)
        held = low_all.at[pl.ds(t * rows, rows), :]
        return pltpu.make_async_remote_copy(
            src_ref=held,
            dst_ref=held,
            send_sem=low_send.at[d],
            recv_sem=low_recv.at[d],
            device_id={"tensor": to},
            device_id_type=MESH,
        )

    def low_arrival(d):
        source = lax.rem(t + n - d, n)
        held = low_all.at[pl.ds(source * rows, rows), :]
        return pltpu.make_async_remote_copy(
            src_ref=held,
            dst_ref=held,
            send_sem=low_send.at[d],
            recv_sem=low_recv.at[d],
            device_id={"tensor": source},
            device_id_type=MESH,
        )

    def adapters_arrive():
        for d in range(1, stores):
            source = lax.rem(s + stores - d, stores)
            for i, (_, held) in enumerate(adapter_pairs):
                block = adapter_block(held, i, source)
                pltpu.make_async_remote_copy(
                    src_ref=block,
                    dst_ref=block,
                    send_sem=adapter_send.at[i, d],
                    recv_sem=adapter_recv.at[i, d],
                    device_id={"store": source},
                    device_id_type=MESH,
                ).wait_recv()

    def low_first():
        fill_holder()
        adapters_arrive()
        summed = jnp.zeros(low_part.shape, jnp.float32)
        for p in range(stores):
            picked = jnp.zeros(low_part.shape, jnp.float32)
            for k in range(share):
                picked += lax.dot_general(
                    xbuf[t * share + k],
                    down[p, :, k * width : (k + 1) * width],
                    (((1,), (1,)), ((), ())),
                    preferred_element_type=jnp.float32,
                )
            summed += picked * mask_of(p)
        low_part[...] = summed.astype(jnp.bfloat16)
        low_own[...] = summed
        for d in range(1, n):
            part_copy(d).start()

    def low_second():
        at = pl.ds(pl.multiple_of(t * rows, rows), rows)
        whole = low_own[at, :]
        for d in range(1, n):
            part_arrival(d).wait_recv()
            whole += low_got[lax.rem(t + n - d, n)].astype(jnp.float32)
        low_all[at, :] = whole.astype(jnp.bfloat16)
        for d in range(1, n):
            low_copy(d).start()

    def low_third():
        for d in range(1, n):
            low_arrival(d).wait_recv()
        low = low_all[...].astype(jnp.float32)
        turned = pltpu.roll(low, ADAPTER_RANK, 1)
        in_lower = lax.broadcasted_iota(jnp.int32, low.shape, 1) < ADAPTER_RANK
        twice_q = jnp.where(in_lower, low, turned)
        twice_kv = jnp.where(in_lower, turned, low)
        masks = [
            jnp.where(in_lower, mask_of(2 * p), mask_of(2 * p + 1))
            for p in range(stores // 2)
        ]
        spread_q = jnp.concatenate([(twice_q * m).astype(jnp.bfloat16) for m in masks], axis=1)
        spread_kv = jnp.concatenate([(twice_kv * m).astype(jnp.bfloat16) for m in masks], axis=1)
        acc_kv[...] += adapter_scale * jnp.dot(
            spread_kv, upkv[...], preferred_element_type=jnp.float32
        )
        for k in range(query_width // tile_q):
            columns = slice(k * tile_q, (k + 1) * tile_q)
            acc_q[:, columns] += adapter_scale * jnp.dot(
                spread_q, upq[:, columns], preferred_element_type=jnp.float32
            )

    def rotated(value, cosine, sine):
        return value * cosine + pltpu.roll(value, HEAD_SIZE // 2, 1) * sine

    ends_first = t >= n - t
    early_start = pl.multiple_of(jnp.where(ends_first, rows, 0), rows)
    late_start = pl.multiple_of(jnp.where(ends_first, 0, total - rows), rows)
    partner = t + 1 - 2 * (t % 2)

    def finish_keyval(start, count):
        at = pl.ds(start, count)
        cosine = jnp.where(holds_keys, cos_ref[at, :], 1.0)
        sine = jnp.where(holds_keys, sin_ref[at, :], 0.0)
        for m in range(pair_heads):
            value = acc_kv[at, m * HEAD_SIZE : (m + 1) * HEAD_SIZE]
            kv_heads[m, at, :] = rotated(value, cosine, sine).astype(jnp.bfloat16)

    def keyval_copy(start, count, which):
        at = pl.ds(start, count)
        return pltpu.make_async_remote_copy(
            src_ref=kv_heads.at[pl.ds(kv_first(partner), kv_used), at, :],
            dst_ref=kv_got.at[:, at, :],
            send_sem=kv_sem.at[0, which],
            recv_sem=kv_sem.at[1, which],
            device_id={"tensor": partner},
            device_id_type=MESH,
        )

    own_first = kv_first(t)
    is_inner = jnp.logical_not(is_end)
    starts_first = jnp.logical_not(ends_first)
    holds_values = jnp.logical_not(holds_keys)
    early_count = total - rows
    per_kv = head_local // kv_used
    batch = min(8, per_kv)
    block = 128
    blocks = total // block
    scale = 1.0 / math.sqrt(HEAD_SIZE) / math.log(2.0)
    stage_at = pl.multiple_of(jnp.where(ends_first, model_width - total, 0), total)
    part_at = pl.multiple_of(jnp.where(ends_first, model_width - 2 * total, total), total)

    def finish_late():
        finish_keyval(late_start, rows)
        keyval_copy(late_start, rows, 1).start()

    def gather_keys(start, count):
        at = pl.ds(start, count)
        for g in range(kv_used):

            @pl.when(holds_keys)
            def _():
                keys_ref[g, at, :] = kv_heads[own_first + g, at, :]

            @pl.when(holds_values)
            def _():
                keys_ref[g, at, :] = kv_got[g, at, :]

    def gather_values(start, count):
        at = pl.ds(start, count)
        for g in range(kv_used):

            @pl.when(holds_keys)
            def _():
                values_ref[g, at, :HEAD_SIZE] = kv_got[g, at, :]

            @pl.when(holds_values)
            def _():
                values_ref[g, at, :HEAD_SIZE] = kv_heads[own_first + g, at, :]

    def lanes_of(h):
        return pl.ds(pl.multiple_of(h * HEAD_SIZE, HEAD_SIZE), HEAD_SIZE)

    def stage_rows(start, first, count):
        return pl.ds(pl.multiple_of(start + first, block), count)

    def weights_of(b, g, lanes):
        low = max(0, b * block - MAX_RUN)
        high = (b + 1) * block
        at = slice(b * block, high)
        query = [
            rotated(acc_q[at, ln], cos_ref[at, :], sin_ref[at, :]).astype(jnp.bfloat16)
            for ln in lanes
        ]
        scores = lax.dot_general(
            jnp.concatenate(query, axis=0),
            keys_ref[g, low:high, :],
            (((1,), (1,)), ((), ())),
            preferred_element_type=jnp.float32,
        )
        scores = scores.reshape(2, block, high - low) + bias_ref[at, low:high][None]
        scores = (scores - jnp.max(scores, axis=2, keepdims=True)) * scale
        return jnp.exp2(scores).astype(jnp.bfloat16).reshape(2 * block, high - low)

    def attend(b, g, lanes):
        low = max(0, b * block - MAX_RUN)
        high = (b + 1) * block
        mixed = jnp.dot(
            weights_of(b, g, lanes), values_ref[g, low:high, :], preferred_element_type=jnp.float32
        )
        mixed = (mixed[:, :HEAD_SIZE] / mixed[:, HEAD_SIZE:]).astype(jnp.bfloat16)
        for k, ln in enumerate(lanes):
            wq[stage_rows(stage_at, b * block, block), ln] = mixed[k * block : (k + 1) * block]

    def attend_part(b, g, lanes):
        high = (b + 1) * block
        weights = weights_of(b, g, lanes)
        first = weights[:, :block]
        mixed = jnp.dot(
            weights[:, block:], values_ref[g, block:high, :], preferred_element_type=jnp.float32
        )
        sums = mixed[:, HEAD_SIZE:] + jnp.dot(
            first, values_ref[g, :block, HEAD_SIZE:], preferred_element_type=jnp.float32
        )
        inverse = 1.0 / sums
        rest = mixed[:, :HEAD_SIZE] * inverse
        first = (first.astype(jnp.float32) * inverse).astype(jnp.bfloat16)
        for k, ln in enumerate(lanes):
            acc_q[b * block : high, ln] = rest[k * block : (k + 1) * block]
            wq[stage_rows(part_at, b * block, block), ln] = first[k * block : (k + 1) * block]

    def attend_rest(g, ln):
        count = (blocks - 2) * block
        more = jnp.dot(
            wq[stage_rows(part_at, block, count), ln],
            values_ref[g, :block, :HEAD_SIZE],
            preferred_element_type=jnp.float32,
        )
        whole = acc_q[block : block + count, ln] + more
        wq[stage_rows(stage_at, block, count), ln] = whole.astype(jnp.bfloat16)

    cut = total - block

    def out_copy(q, which):
        first, count = (0, cut) if which == 0 else (cut, block)
        lanes = pl.ds(pl.multiple_of(q * batch * HEAD_SIZE, batch * HEAD_SIZE), batch * HEAD_SIZE)
        return pltpu.make_async_copy(
            wq.at[stage_rows(stage_at, first, count), lanes],
            out_ref.at[pl.ds(first, count), lanes],
            out_sem.at[which, q],
        )

    def heads(body, which, q):
        g = q * batch // per_kv
        for pair in range(batch // 2):
            body(g, [lanes_of(q * batch + 2 * pair + k) for k in range(2)])
        out_copy(q, which).start()

    def over_heads(body, which):
        @pl.loop(0, head_local // batch)
        def _(q):
            heads(body, which, q)

    def early_keyval():
        keyval_copy(early_start, early_count, 0).wait_recv()
        gather_keys(early_start, early_count)
        gather_values(early_start, early_count)

        @pl.when(ends_first)
        def _():
            @pl.when(holds_values)
            def _():
                keyval_copy(late_start, rows, 1).wait_recv()

            gather_keys(late_start, rows)

    def early_attention(q):
        @pl.when(starts_first)
        def _():
            def body(g, lanes):
                for b in range(blocks - 1):
                    attend(b, g, lanes)

            heads(body, 0, q)

        @pl.when(ends_first)
        def _():
            def body(g, lanes):
                attend(blocks - 1, g, lanes)
                for b in range(1, blocks - 1):
                    attend_part(b, g, lanes)

            heads(body, 1, q)

    def late_attention():
        @pl.when(starts_first)
        def _():
            keyval_copy(late_start, rows, 1).wait_recv()
            gather_keys(late_start, rows)
            gather_values(late_start, rows)

            def body(g, lanes):
                attend(blocks - 1, g, lanes)

            over_heads(body, 1)

        @pl.when(ends_first)
        def _():
            @pl.when(holds_keys)
            def _():
                keyval_copy(late_start, rows, 1).wait_recv()

            gather_values(late_start, rows)

            def body(g, lanes):
                attend(0, g, lanes)
                for ln in lanes:
                    attend_rest(g, ln)

            over_heads(body, 0)

    for g in range(kv_used):
        values_ref[g, :, HEAD_SIZE:] = jnp.ones((total, HEAD_SIZE), jnp.bfloat16)

    @pl.loop(0, (n - 1) * chunks)
    def _(step):
        here = tuple(step < reach[side] * chunks for side in range(2))
        places = [item(reach[side], step) for side in range(2)]
        for side in range(2):
            p, i = places[side]

            @pl.when(here[side])
            def _():
                arrival(side, p, i).wait_recv()

            sends = (reach[side] + 1) * chunks
            head = (reach[side] + 1) * share

            @pl.when(jnp.logical_and(can_send[side], step + depth < sends))
            def _():
                send_item(side, step, False).wait_send()

                @pl.when(step + ahead <= head)
                def _():
                    start_send(side, step + ahead)

                @pl.when(step + ahead == head)
                def _():
                    for j in range(1, depth - 1):
                        start_send(side, step + ahead + j)

                @pl.when(step + ahead > head)
                def _():
                    start_send(side, step + depth)

        @pl.when(step < chunks // 2)
        def _():
            for c in (step, chunks - 1 - step):
                for copy in weight_copies(c):
                    copy.wait()

            @pl.when(step + 1 < chunks // 2)
            def _():
                start_weights(step + 1)

        for side in range(2):
            p, i = places[side]

            @pl.when(here[side])
            def _():
                keyval_unit(place(side, i), t - p if side == 0 else t + p)

        @pl.when(jnp.logical_and(is_end, step == last_step))
        def _():
            finish_late()

        for side in range(2):
            p, i = places[side]

            @pl.when(here[side])
            def _():
                query_unit(place(side, i), t - p if side == 0 else t + p)

        @pl.when(jnp.logical_and(step >= chunks, step < 2 * chunks))
        def _():
            keyval_unit(step - chunks, t)
            query_unit(step - chunks, t)

        @pl.when(step == chunks - 2)
        def _():
            fill_tables()

        @pl.when(step == low_at)
        def _():
            low_first()

        @pl.when(step == second_at)
        def _():
            low_second()

        @pl.when(step == third_at)
        def _():
            low_third()

        @pl.when(step == third_at)
        def _():
            finish_keyval(early_start, early_count)
            keyval_copy(early_start, early_count, 0).start()

            @pl.when(is_inner)
            def _():
                finish_late()

        @pl.when(step == early_at)
        def _():
            early_keyval()

        @pl.when(jnp.logical_and(step >= early_at, step < early_at + head_local // batch))
        def _():
            early_attention(step - early_at)

    late_attention()

    for copy in adapter_sends:
        copy.wait_send()
    for d in range(1, n):
        part_copy(d).wait_send()
        low_copy(d).wait_send()
    keyval_copy(early_start, early_count, 0).wait_send()
    keyval_copy(late_start, rows, 1).wait_send()

    for side in range(2):

        @pl.when(can_send[side])
        def _():
            for j in range(depth):
                send_item(side, (reach[side] + 1) * chunks - depth + j, False).wait_send()

    @pl.loop(0, head_local // batch)
    def _(q):
        for which in range(2):
            out_copy(q, which).wait()


def on_device(
    tokens,
    query_weight,
    key_value_weight,
    adapter_down_maps,
    adapter_up_query,
    adapter_up_key_value,
    adapter_row_table,
    request_adapter_ids,
    token_request_ids,
):
    n = lax.axis_size("tensor")
    stores = lax.axis_size("store")
    slots = adapter_down_maps.shape[0]
    rows, model_width = tokens.shape
    total = rows * n
    query_width = query_weight.shape[1]
    keyval_width = key_value_weight.shape[1]
    chunks = max(8, 2 * n)
    width = model_width // chunks
    pair_heads = keyval_width // HEAD_SIZE
    kv_used = max(query_width // HEAD_SIZE // (QUERY_HEADS // KEY_VALUE_HEADS), 1)
    two_ranks = 2 * ADAPTER_RANK
    hbm = pl.BlockSpec(memory_space=pl.ANY)
    vmem = pl.BlockSpec(memory_space=pltpu.VMEM)
    smem = pl.BlockSpec(memory_space=pltpu.SMEM)
    dma = pltpu.SemaphoreType.DMA
    return pl.pallas_call(
        functools.partial(project_kernel, n, stores, chunks, slots),
        in_specs=[hbm] * 6 + [smem, smem, vmem],
        out_specs=[hbm] * 4,
        out_shape=[
            jax.ShapeDtypeStruct((total, query_width), jnp.bfloat16),
            jax.ShapeDtypeStruct((stores, two_ranks, query_width), jnp.bfloat16),
            jax.ShapeDtypeStruct((stores, ADAPTER_RANK, query_width), jnp.bfloat16),
            jax.ShapeDtypeStruct((stores, ADAPTER_RANK, keyval_width), jnp.bfloat16),
        ],
        scratch_shapes=[
            pltpu.VMEM((chunks, total, width), jnp.bfloat16),
            pltpu.VMEM((model_width, query_width), jnp.bfloat16),
            pltpu.VMEM((model_width, keyval_width), jnp.bfloat16),
            pltpu.VMEM((total, query_width), jnp.float32),
            pltpu.VMEM((total, keyval_width), jnp.float32),
            pltpu.VMEM((stores, two_ranks, model_width // n), jnp.bfloat16),
            pltpu.VMEM((stores * ADAPTER_RANK, query_width), jnp.bfloat16),
            pltpu.VMEM((stores * ADAPTER_RANK, keyval_width), jnp.bfloat16),
            pltpu.VMEM((total, two_ranks), jnp.bfloat16),
            pltpu.VMEM((total, two_ranks), jnp.float32),
            pltpu.VMEM((n, rows, two_ranks), jnp.bfloat16),
            pltpu.VMEM((total, two_ranks), jnp.bfloat16),
            pltpu.VMEM((pair_heads, total, HEAD_SIZE), jnp.bfloat16),
            pltpu.VMEM((kv_used, total, HEAD_SIZE), jnp.bfloat16),
            pltpu.VMEM((kv_used, total, HEAD_SIZE), jnp.bfloat16),
            pltpu.VMEM((kv_used, total, 2 * HEAD_SIZE), jnp.bfloat16),
            pltpu.VMEM((total, total), jnp.float32),
            pltpu.VMEM((total, HEAD_SIZE), jnp.float32),
            pltpu.VMEM((total, HEAD_SIZE), jnp.float32),
            pltpu.VMEM((total, 1), jnp.float32),
            dma((chunks,)),
            dma((2, chunks)),
            dma((2, n, chunks)),
            dma((2, n, chunks)),
            dma((3, stores)),
            dma((3, stores)),
            dma((3,)),
            dma((3, slots)),
            dma((3, stores)),
            dma((n,)),
            dma((n,)),
            dma((n,)),
            dma((n,)),
            dma((2, 2)),
            dma((2, query_width // HEAD_SIZE)),
        ],
        compiler_params=pltpu.CompilerParams(
            collective_id=0, has_side_effects=True, vmem_limit_bytes=67043328
        ),
        name="project",
    )(
        tokens,
        query_weight,
        key_value_weight,
        adapter_down_maps,
        adapter_up_query,
        adapter_up_key_value,
        adapter_row_table,
        request_adapter_ids,
        token_request_ids,
    )[0]


def solution(mesh):
    return jax.shard_map(
        on_device,
        mesh=mesh,
        in_specs=(
            P(("groups", "store", "tensor"), None),
            P(None, "tensor"),
            P(None, "tensor"),
            P("store", None, "tensor"),
            P("store", None, "tensor"),
            P("store", None, "tensor"),
            P("groups"),
            P("groups", None),
            P(("groups", "store"), None),
        ),
        out_specs=P(("groups", "store"), "tensor"),
        check_vma=False,
    )
```

```python
import functools
import math

import jax
import jax.numpy as jnp
from jax import lax
from jax.experimental import pallas as pl
from jax.experimental.pallas import tpu as pltpu
from jax.sharding import PartitionSpec as P

MODEL_WIDTH = 8192
QUERY_HEADS = 64
KEY_VALUE_HEADS = 8
HEAD_SIZE = 128
ADAPTER_RANK = 64
STORE_REQUESTS = 4
TOK_ST = 512


adapter_scale = 2.0
rope_theta = 500000.0


MAX_RUN = 256
MESH = pl.DeviceIdType.MESH


def project_kernel(
    n,
    stores,
    chunks,
    slots,
    tokens_ref,
    wq_hbm,
    wkv_hbm,
    down_hbm,
    upq_hbm,
    upkv_hbm,
    table_ref,
    request_ref,
    segment_ref,
    out_ref,
    down_picked,
    upq_picked,
    upkv_picked,
    xbuf,
    wq,
    wkv,
    acc_q,
    acc_kv,
    down,
    upq,
    upkv,
    low_part,
    low_own,
    low_got,
    low_all,
    kv_heads,
    kv_got,
    keys_ref,
    values_ref,
    bias_ref,
    cos_ref,
    sin_ref,
    holder_ref,
    token_sem,
    weight_sem,
    recv_sem,
    send_sem,
    adapter_send,
    adapter_recv,
    adapter_own,
    candidate_sem,
    picked_sem,
    part_send,
    part_recv,
    low_send,
    low_recv,
    kv_sem,
    out_sem,
):
    t = lax.axis_index("tensor")
    s = lax.axis_index("store")
    rows = tokens_ref.shape[0]
    width = tokens_ref.shape[1] // chunks
    total = rows * n
    query_width = wq.shape[1]
    keyval_width = wkv.shape[1]
    pair_heads = keyval_width // HEAD_SIZE
    head_local = query_width // HEAD_SIZE
    group_size = QUERY_HEADS // KEY_VALUE_HEADS
    kv_used = max(head_local // group_size, 1)

    def kv_first(rank):
        return rank * head_local // group_size - rank // 2 * pair_heads

    barrier = pltpu.get_barrier_semaphore()
    for d in range(1, n):
        pl.semaphore_signal(
            barrier, inc=1, device_id={"tensor": lax.rem(t + d, n)}, device_id_type=MESH
        )
    for d in range(1, stores):
        pl.semaphore_signal(
            barrier, inc=1, device_id={"store": lax.rem(s + d, stores)}, device_id_type=MESH
        )

    def own_copy(c):
        return pltpu.make_async_copy(
            tokens_ref.at[:, pl.ds(c * width, width)],
            xbuf.at[c, pl.ds(t * rows, rows), :],
            token_sem.at[c],
        )

    def weight_copies(c):
        part = pl.ds(c * width, width)
        return (
            pltpu.make_async_copy(wq_hbm.at[part, :], wq.at[part, :], weight_sem.at[0, c]),
            pltpu.make_async_copy(wkv_hbm.at[part, :], wkv.at[part, :], weight_sem.at[1, c]),
        )

    model_width = wq.shape[0]
    two_ranks = 2 * ADAPTER_RANK
    picked_down = chunks // 2 * width
    picked_up = picked_down + stores * two_ranks
    picked_end = picked_up + stores * ADAPTER_RANK
    candidate_sets = (
        (down_hbm, wq, 0, two_ranks, picked_down, down_picked),
        (upq_hbm, wq, slots * two_ranks, ADAPTER_RANK, picked_up, upq_picked),
        (upkv_hbm, wkv, 0, ADAPTER_RANK, picked_up, upkv_picked),
    )
    candidates = [
        pltpu.make_async_copy(
            source.at[k], held.at[pl.ds(first + k * count, count), :], candidate_sem.at[j, k]
        )
        for j, (source, held, first, count, _, _) in enumerate(candidate_sets)
        for k in range(slots)
    ]
    adapter_pairs = ((down_picked, down), (upq_picked, upq), (upkv_picked, upkv))

    def adapter_block(held, i, at):
        if i == 0:
            return held.at[at]
        return held.at[pl.ds(at * ADAPTER_RANK, ADAPTER_RANK), :]

    own_adapters = [
        pltpu.make_async_copy(source.at[s], adapter_block(held, i, s), adapter_own.at[i])
        for i, (source, held) in enumerate(adapter_pairs)
    ]

    pl.semaphore_wait(barrier, n - 1 + stores - 1)

    def place(side, i):
        return chunks - 1 - i if side == 0 else i

    def stream_copy(side, p, i, own):
        c = place(side, i)
        shard = t - p if side == 0 else t + p
        held = xbuf.at[c, pl.ds(shard * rows, rows), :]
        source = tokens_ref.at[:, pl.ds(c * width, width)] if own else held
        return pltpu.make_async_remote_copy(
            src_ref=source,
            dst_ref=held,
            send_sem=send_sem.at[side, p, i],
            recv_sem=recv_sem.at[side, p, i],
            device_id={"tensor": t + 1 if side == 0 else t - 1},
            device_id_type=MESH,
        )

    def arrival(side, p, i):
        c = place(side, i)
        shard = t - p if side == 0 else t + p
        held = xbuf.at[c, pl.ds(shard * rows, rows), :]
        return pltpu.make_async_remote_copy(
            src_ref=held,
            dst_ref=held,
            send_sem=send_sem.at[side, p - 1, i],
            recv_sem=recv_sem.at[side, p - 1, i],
            device_id={"tensor": t - 1 if side == 0 else t + 1},
            device_id_type=MESH,
        )

    is_end = jnp.logical_or(t == 0, t == n - 1)
    share = chunks // n
    can_send = (t < n - 1, t > 0)
    reach = (t, n - 1 - t)

    def item(shards, j):
        head = share * shards
        rest = chunks - share
        in_head = j < head
        k = jnp.maximum(j - head, 0)
        return (
            jnp.where(in_head, j // share, k // rest) + 1,
            jnp.where(in_head, j % share, share + k % rest),
        )

    def send_item(side, j, own):
        p, i = item(reach[side] + 1, j)
        return stream_copy(side, p - 1, i, own)

    def start_send(side, j):
        p, i = item(reach[side] + 1, j)

        @pl.when(p == 1)
        def _():
            stream_copy(side, 0, i, True).start()

        @pl.when(p > 1)
        def _():
            stream_copy(side, p - 1, i, False).start()

    ahead = 2
    depth = 4
    for j in range(ahead):
        for side in range(2):

            @pl.when(can_send[side])
            def _():
                stream_copy(side, 0, j, True).start()

    for copy in candidates:
        copy.start()
    for c in range(chunks):
        own_copy(c).start()

    tile_q = min(query_width, 512)

    def keyval_unit(c, shard):
        at = pl.ds(pl.multiple_of(shard * rows, rows), rows)
        part = pl.ds(pl.multiple_of(c * width, width), width)
        acc_kv[at, :] += jnp.dot(
            xbuf[c, at, :], wkv[part, :], preferred_element_type=jnp.float32
        )

    def query_unit(c, shard):
        at = pl.ds(pl.multiple_of(shard * rows, rows), rows)
        part = pl.ds(pl.multiple_of(c * width, width), width)

        @pl.loop(0, query_width // tile_q)
        def _(k):
            columns = pl.ds(pl.multiple_of(k * tile_q, tile_q), tile_q)
            acc_q[at, columns] += jnp.dot(
                xbuf[c, at, :], wq[part, columns], preferred_element_type=jnp.float32
            )

    acc_q[...] = jnp.zeros_like(acc_q)
    acc_kv[...] = jnp.zeros_like(acc_kv)
    holds_keys = t % 2 == 0

    def request_column():
        place_row = lax.broadcasted_iota(jnp.int32, (total, total), 0)
        place_column = lax.broadcasted_iota(jnp.int32, (total, total), 1)
        across = segment_ref[...].astype(jnp.float32)
        own = jnp.where(place_row == place_column, across, 0.0)
        return across, jnp.sum(own, axis=1, keepdims=True), place_row >= place_column

    def fill_tables():
        across, down_column, ordered = request_column()
        allowed = jnp.logical_and(down_column == across, ordered)
        bias_ref[...] = jnp.where(allowed, 0.0, -1e30)
        first_index = jnp.sum(jnp.where(across < down_column, 1.0, 0.0), axis=1, keepdims=True)
        place_token = lax.broadcasted_iota(jnp.int32, (total, 1), 0).astype(jnp.float32)
        lane = lax.broadcasted_iota(jnp.int32, (total, HEAD_SIZE), 1)
        exponent = lax.rem(lane, HEAD_SIZE // 2).astype(jnp.float32) * (2.0 / HEAD_SIZE)
        angles = (place_token - first_index) * jnp.exp(-exponent * math.log(rope_theta))
        sine = jnp.sin(angles)
        cos_ref[...] = jnp.cos(angles)
        sin_ref[...] = jnp.where(lane < HEAD_SIZE // 2, -sine, sine)

    def fill_holder():
        _, down_column, _ = request_column()
        holder = jnp.zeros((total, 1), jnp.float32)
        for k in range(STORE_REQUESTS):
            owner = lax.div(table_ref[request_ref[s, k]], slots).astype(jnp.float32)
            holder += jnp.where(down_column == float(k), owner, 0.0)
        holder_ref[...] = holder

    for copy in candidates:
        copy.wait()
    bits = []
    for i in range(stores):
        index = 0
        for k in range(STORE_REQUESTS):
            slot = table_ref[request_ref[i, k]]
            index += jnp.where(lax.div(slot, slots) == s, lax.rem(slot, slots), 0)
        bits.append([lax.rem(lax.div(index, 1 << k), 2) == 1 for k in range(slots.bit_length())])

    def pick(held, first, count, to):
        lanes = min(held.shape[1], 512)

        @pl.loop(0, count // 16)
        def _(r):
            for at in range(0, held.shape[1], lanes):
                columns = slice(at, at + lanes)

                def tile(base, k):
                    return pl.ds(pl.multiple_of(base + k * count + r * 16, 16), 16)

                found = [held[tile(first, k), columns] for k in range(slots)]
                for i in range(stores):
                    left, level = found, 0
                    while len(left) > 1:
                        bit = bits[i][level]
                        left = [
                            jnp.where(bit, left[k + 1], left[k]) if k + 1 < len(left) else left[k]
                            for k in range(0, len(left), 2)
                        ]
                        level += 1
                    held[tile(to, i), columns] = left[0]

    for _, held, first, count, to, _ in candidate_sets:
        pick(held, first, count, to)
    picked_copies = [
        pltpu.make_async_copy(
            held.at[pl.ds(to + i * count, count), :], picked.at[i], picked_sem.at[j, i]
        )
        for j, (_, held, _, count, to, picked) in enumerate(candidate_sets)
        for i in range(stores)
    ]
    for copy in picked_copies:
        copy.start()
    def start_weights(k):
        for c in (k, chunks - 1 - k):
            for copy in weight_copies(c):
                copy.start()

    start_weights(0)
    for copy in picked_copies:
        copy.wait()
    for copy in own_adapters:
        copy.start()
    adapter_sends = []
    for d in range(1, stores):
        for i, (source, held) in enumerate(adapter_pairs):
            peer = lax.rem(s + d, stores)
            copy = pltpu.make_async_remote_copy(
                src_ref=source.at[peer],
                dst_ref=adapter_block(held, i, s),
                send_sem=adapter_send.at[i, d],
                recv_sem=adapter_recv.at[i, d],
                device_id={"store": peer},
                device_id_type=MESH,
            )
            copy.start()
            adapter_sends.append(copy)


    def mask_of(p):
        return jnp.where(holder_ref[...] == float(p), 1.0, 0.0)

    for copy in own_adapters:
        copy.wait()
    for c in range(chunks):
        own_copy(c).wait()

    def low_ready(side):
        first = share * (t if side == 1 else n - 1 - t)
        i = first + share - 1
        shards = reach[side]
        in_rest = share * shards + (shards - 1) * (chunks - share) + i - share
        return jnp.where(shards == 0, 0, jnp.where(i < share, share * shards - 1, in_rest))

    last_step = (n - 1) * chunks - 1
    inner_done = (n - 2) * chunks - 1
    third_at = jnp.where(is_end, last_step - 4, inner_done + 1)
    early_at = last_step - jnp.where(is_end, 4, 3)
    low_at = jnp.maximum(jnp.maximum(low_ready(0), low_ready(1)), chunks)

    pairs = n // 2
    owners = [2 * m + 1 if 2 * m + 1 < n - 2 * m - 1 else 2 * m for m in range(pairs)]
    own_pair = t // 2
    is_owner = t == 2 * own_pair + jnp.where(2 * own_pair + 1 < n - 2 * own_pair - 1, 1, 0)

    def pair_rows(m):
        start = m * 2 * rows
        return pl.ds(start if isinstance(m, int) else pl.multiple_of(start, 2 * rows), 2 * rows)

    def part_copy(m):
        return pltpu.make_async_remote_copy(
            src_ref=low_part.at[pair_rows(m), :],
            dst_ref=low_got.at[t],
            send_sem=part_send.at[m],
            recv_sem=part_recv.at[t],
            device_id={"tensor": owners[m]},
            device_id_type=MESH,
        )

    def part_arrival(d):
        source = lax.rem(t + n - d, n)
        return pltpu.make_async_remote_copy(
            src_ref=low_got.at[source],
            dst_ref=low_got.at[source],
            send_sem=part_send.at[0],
            recv_sem=part_recv.at[source],
            device_id={"tensor": source},
            device_id_type=MESH,
        )

    def low_copy(d):
        held = low_all.at[pair_rows(own_pair), :]
        return pltpu.make_async_remote_copy(
            src_ref=held,
            dst_ref=held,
            send_sem=low_send.at[d],
            recv_sem=low_recv.at[own_pair],
            device_id={"tensor": lax.rem(t + d, n)},
            device_id_type=MESH,
        )

    def low_arrival(m):
        held = low_all.at[pair_rows(m), :]
        return pltpu.make_async_remote_copy(
            src_ref=held,
            dst_ref=held,
            send_sem=low_send.at[0],
            recv_sem=low_recv.at[m],
            device_id={"tensor": owners[m]},
            device_id_type=MESH,
        )

    def adapters_arrive():
        for d in range(1, stores):
            source = lax.rem(s + stores - d, stores)
            for i, (_, held) in enumerate(adapter_pairs):
                block = adapter_block(held, i, source)
                pltpu.make_async_remote_copy(
                    src_ref=block,
                    dst_ref=block,
                    send_sem=adapter_send.at[i, d],
                    recv_sem=adapter_recv.at[i, d],
                    device_id={"store": source},
                    device_id_type=MESH,
                ).wait_recv()

    def low_first():
        fill_holder()
        adapters_arrive()
        summed = jnp.zeros(low_part.shape, jnp.float32)
        for p in range(stores):
            picked = jnp.zeros(low_part.shape, jnp.float32)
            for k in range(share):
                picked += lax.dot_general(
                    xbuf[t * share + k],
                    down[p, :, k * width : (k + 1) * width],
                    (((1,), (1,)), ((), ())),
                    preferred_element_type=jnp.float32,
                )
            summed += picked * mask_of(p)
        low_part[...] = summed.astype(jnp.bfloat16)
        low_own[...] = summed
        for m in range(pairs):

            @pl.when(t != owners[m])
            def _():
                part_copy(m).start()

    def low_second():
        at = pair_rows(own_pair)
        whole = low_own[at, :]
        for d in range(1, n):
            part_arrival(d).wait_recv()
            whole += low_got[lax.rem(t + n - d, n)].astype(jnp.float32)
        low_all[at, :] = whole.astype(jnp.bfloat16)
        for d in range(1, n):
            low_copy(d).start()

    def spread_low(lower):
        low = low_all[...].astype(jnp.float32)
        turned = pltpu.roll(low, ADAPTER_RANK, 1)
        in_lower = lax.broadcasted_iota(jnp.int32, low.shape, 1) < ADAPTER_RANK
        twice = jnp.where(in_lower, low, turned) if lower else jnp.where(in_lower, turned, low)
        masks = [
            jnp.where(in_lower, mask_of(2 * p), mask_of(2 * p + 1)) for p in range(stores // 2)
        ]
        return jnp.concatenate([(twice * m).astype(jnp.bfloat16) for m in masks], axis=1)

    def low_keyval():
        for m in range(pairs):

            @pl.when(t != owners[m])
            def _():
                low_arrival(m).wait_recv()

        acc_kv[...] += adapter_scale * jnp.dot(
            spread_low(False), upkv[...], preferred_element_type=jnp.float32
        )

    def low_query():
        spread = spread_low(True)
        for k in range(query_width // tile_q):
            columns = slice(k * tile_q, (k + 1) * tile_q)
            acc_q[:, columns] += adapter_scale * jnp.dot(
                spread, upq[:, columns], preferred_element_type=jnp.float32
            )

    def rotated(value, cosine, sine):
        return value * cosine + pltpu.roll(value, HEAD_SIZE // 2, 1) * sine

    ends_first = t >= n - t
    early_start = pl.multiple_of(jnp.where(ends_first, rows, 0), rows)
    late_start = pl.multiple_of(jnp.where(ends_first, 0, total - rows), rows)
    partner = t + 1 - 2 * (t % 2)

    def finish_keyval(start, count):
        at = pl.ds(start, count)
        cosine = jnp.where(holds_keys, cos_ref[at, :], 1.0)
        sine = jnp.where(holds_keys, sin_ref[at, :], 0.0)
        for m in range(pair_heads):
            value = acc_kv[at, m * HEAD_SIZE : (m + 1) * HEAD_SIZE]
            kv_heads[m, at, :] = rotated(value, cosine, sine).astype(jnp.bfloat16)

    def keyval_copy(start, count, which):
        at = pl.ds(start, count)
        return pltpu.make_async_remote_copy(
            src_ref=kv_heads.at[pl.ds(kv_first(partner), kv_used), at, :],
            dst_ref=kv_got.at[:, at, :],
            send_sem=kv_sem.at[0, which],
            recv_sem=kv_sem.at[1, which],
            device_id={"tensor": partner},
            device_id_type=MESH,
        )

    own_first = kv_first(t)
    is_inner = jnp.logical_not(is_end)
    starts_first = jnp.logical_not(ends_first)
    holds_values = jnp.logical_not(holds_keys)
    early_count = total - rows
    per_kv = head_local // kv_used
    batch = min(8, per_kv)
    block = 128
    blocks = total // block
    scale = 1.0 / math.sqrt(HEAD_SIZE) / math.log(2.0)
    stage_at = pl.multiple_of(jnp.where(ends_first, model_width - total, 0), total)
    part_at = pl.multiple_of(jnp.where(ends_first, model_width - 2 * total, total), total)

    def finish_late():
        finish_keyval(late_start, rows)
        keyval_copy(late_start, rows, 1).start()

    def gather_keys(start, count):
        at = pl.ds(start, count)
        for g in range(kv_used):

            @pl.when(holds_keys)
            def _():
                keys_ref[g, at, :] = kv_heads[own_first + g, at, :]

            @pl.when(holds_values)
            def _():
                keys_ref[g, at, :] = kv_got[g, at, :]

    def gather_values(start, count):
        at = pl.ds(start, count)
        for g in range(kv_used):

            @pl.when(holds_keys)
            def _():
                values_ref[g, at, :HEAD_SIZE] = kv_got[g, at, :]

            @pl.when(holds_values)
            def _():
                values_ref[g, at, :HEAD_SIZE] = kv_heads[own_first + g, at, :]

    def lanes_of(h):
        return pl.ds(pl.multiple_of(h * HEAD_SIZE, HEAD_SIZE), HEAD_SIZE)

    def stage_rows(start, first, count):
        return pl.ds(pl.multiple_of(start + first, block), count)

    def weights_of(b, g, lanes):
        low = max(0, b * block - MAX_RUN)
        high = (b + 1) * block
        at = slice(b * block, high)
        query = [
            rotated(acc_q[at, ln], cos_ref[at, :], sin_ref[at, :]).astype(jnp.bfloat16)
            for ln in lanes
        ]
        scores = lax.dot_general(
            jnp.concatenate(query, axis=0),
            keys_ref[g, low:high, :],
            (((1,), (1,)), ((), ())),
            preferred_element_type=jnp.float32,
        )
        scores = scores.reshape(2, block, high - low) + bias_ref[at, low:high][None]
        scores = (scores - jnp.max(scores, axis=2, keepdims=True)) * scale
        return jnp.exp2(scores).astype(jnp.bfloat16).reshape(2 * block, high - low)

    def attend(b, g, lanes):
        low = max(0, b * block - MAX_RUN)
        high = (b + 1) * block
        mixed = jnp.dot(
            weights_of(b, g, lanes), values_ref[g, low:high, :], preferred_element_type=jnp.float32
        )
        mixed = (mixed[:, :HEAD_SIZE] / mixed[:, HEAD_SIZE:]).astype(jnp.bfloat16)
        for k, ln in enumerate(lanes):
            wq[stage_rows(stage_at, b * block, block), ln] = mixed[k * block : (k + 1) * block]

    def attend_part(b, g, lanes):
        high = (b + 1) * block
        weights = weights_of(b, g, lanes)
        first = weights[:, :block]
        mixed = jnp.dot(
            weights[:, block:], values_ref[g, block:high, :], preferred_element_type=jnp.float32
        )
        sums = mixed[:, HEAD_SIZE:] + jnp.dot(
            first, values_ref[g, :block, HEAD_SIZE:], preferred_element_type=jnp.float32
        )
        inverse = 1.0 / sums
        rest = mixed[:, :HEAD_SIZE] * inverse
        first = (first.astype(jnp.float32) * inverse).astype(jnp.bfloat16)
        for k, ln in enumerate(lanes):
            acc_q[b * block : high, ln] = rest[k * block : (k + 1) * block]
            wq[stage_rows(part_at, b * block, block), ln] = first[k * block : (k + 1) * block]

    def attend_rest(g, ln):
        count = (blocks - 2) * block
        more = jnp.dot(
            wq[stage_rows(part_at, block, count), ln],
            values_ref[g, :block, :HEAD_SIZE],
            preferred_element_type=jnp.float32,
        )
        whole = acc_q[block : block + count, ln] + more
        wq[stage_rows(stage_at, block, count), ln] = whole.astype(jnp.bfloat16)

    cut = total - block

    def out_copy(q, which):
        first, count = (0, cut) if which == 0 else (cut, block)
        lanes = pl.ds(pl.multiple_of(q * batch * HEAD_SIZE, batch * HEAD_SIZE), batch * HEAD_SIZE)
        return pltpu.make_async_copy(
            wq.at[stage_rows(stage_at, first, count), lanes],
            out_ref.at[pl.ds(first, count), lanes],
            out_sem.at[which, q],
        )

    def heads(body, which, q):
        g = q * batch // per_kv
        for pair in range(batch // 2):
            body(g, [lanes_of(q * batch + 2 * pair + k) for k in range(2)])
        out_copy(q, which).start()

    def over_heads(body, which):
        @pl.loop(0, head_local // batch)
        def _(q):
            heads(body, which, q)

    def early_keyval():
        keyval_copy(early_start, early_count, 0).wait_recv()
        gather_keys(early_start, early_count)
        gather_values(early_start, early_count)

        @pl.when(ends_first)
        def _():
            @pl.when(holds_values)
            def _():
                keyval_copy(late_start, rows, 1).wait_recv()

            gather_keys(late_start, rows)

    def early_attention(q):
        @pl.when(starts_first)
        def _():
            def body(g, lanes):
                for b in range(blocks - 1):
                    attend(b, g, lanes)

            heads(body, 0, q)

        @pl.when(ends_first)
        def _():
            def body(g, lanes):
                attend(blocks - 1, g, lanes)
                for b in range(1, blocks - 1):
                    attend_part(b, g, lanes)

            heads(body, 1, q)

    def late_attention():
        @pl.when(starts_first)
        def _():
            keyval_copy(late_start, rows, 1).wait_recv()
            gather_keys(late_start, rows)
            gather_values(late_start, rows)

            def body(g, lanes):
                attend(blocks - 1, g, lanes)

            over_heads(body, 1)

        @pl.when(ends_first)
        def _():
            @pl.when(holds_keys)
            def _():
                keyval_copy(late_start, rows, 1).wait_recv()

            gather_values(late_start, rows)

            def body(g, lanes):
                attend(0, g, lanes)
                for ln in lanes:
                    attend_rest(g, ln)

            over_heads(body, 0)

    for g in range(kv_used):
        values_ref[g, :, HEAD_SIZE:] = jnp.ones((total, HEAD_SIZE), jnp.bfloat16)

    @pl.loop(0, (n - 1) * chunks)
    def _(step):
        here = tuple(step < reach[side] * chunks for side in range(2))
        places = [item(reach[side], step) for side in range(2)]
        for side in range(2):
            p, i = places[side]

            @pl.when(here[side])
            def _():
                arrival(side, p, i).wait_recv()

            sends = (reach[side] + 1) * chunks
            head = (reach[side] + 1) * share

            @pl.when(jnp.logical_and(can_send[side], step + depth - 1 < sends))
            def _():
                send_item(side, step, False).wait_send()

                @pl.when(step + ahead <= head)
                def _():
                    start_send(side, step + ahead)

                @pl.when(step + ahead == head)
                def _():
                    for j in range(1, depth - 1):
                        start_send(side, step + ahead + j)

                nearer = step > inner_done
                later = step + depth - jnp.where(nearer, 1, 0)
                wanted = jnp.logical_and(step + ahead > head, step != inner_done + 1)

                @pl.when(jnp.logical_and(wanted, later < sends))
                def _():
                    start_send(side, later)

        @pl.when(step < chunks // 2)
        def _():
            for c in (step, chunks - 1 - step):
                for copy in weight_copies(c):
                    copy.wait()

            @pl.when(step + 1 < chunks // 2)
            def _():
                start_weights(step + 1)

        for side in range(2):
            p, i = places[side]

            @pl.when(here[side])
            def _():
                keyval_unit(place(side, i), t - p if side == 0 else t + p)

        @pl.when(jnp.logical_and(is_end, step == last_step))
        def _():
            finish_late()

        for side in range(2):
            p, i = places[side]

            @pl.when(here[side])
            def _():
                query_unit(place(side, i), t - p if side == 0 else t + p)

        @pl.when(jnp.logical_and(step >= chunks, step < 2 * chunks))
        def _():
            keyval_unit(step - chunks, t)
            query_unit(step - chunks, t)

        @pl.when(step == chunks - 2)
        def _():
            fill_tables()

        @pl.when(step == low_at)
        def _():
            low_first()

        @pl.when(jnp.logical_and(is_owner, step == inner_done))
        def _():
            low_second()

        @pl.when(step == third_at)
        def _():
            low_keyval()
            finish_keyval(early_start, early_count)
            keyval_copy(early_start, early_count, 0).start()

            @pl.when(is_inner)
            def _():
                finish_late()

            low_query()

        @pl.when(step == early_at)
        def _():
            early_keyval()

        @pl.when(jnp.logical_and(step >= early_at, step < early_at + head_local // batch))
        def _():
            early_attention(step - early_at)

    late_attention()

    for copy in adapter_sends:
        copy.wait_send()
    for m in range(pairs):

        @pl.when(t != owners[m])
        def _():
            part_copy(m).wait_send()

    @pl.when(is_owner)
    def _():
        for d in range(1, n):
            low_copy(d).wait_send()

    keyval_copy(early_start, early_count, 0).wait_send()
    keyval_copy(late_start, rows, 1).wait_send()

    for side in range(2):

        @pl.when(can_send[side])
        def _():
            for j in range(1, depth):
                send_item(side, (reach[side] + 1) * chunks - depth + j, False).wait_send()

    @pl.loop(0, head_local // batch)
    def _(q):
        for which in range(2):
            out_copy(q, which).wait()


def on_device(
    tokens,
    query_weight,
    key_value_weight,
    adapter_down_maps,
    adapter_up_query,
    adapter_up_key_value,
    adapter_row_table,
    request_adapter_ids,
    token_request_ids,
):
    n = lax.axis_size("tensor")
    stores = lax.axis_size("store")
    slots = adapter_down_maps.shape[0]
    rows, model_width = tokens.shape
    total = rows * n
    query_width = query_weight.shape[1]
    keyval_width = key_value_weight.shape[1]
    chunks = max(8, 2 * n)
    width = model_width // chunks
    pair_heads = keyval_width // HEAD_SIZE
    kv_used = max(query_width // HEAD_SIZE // (QUERY_HEADS // KEY_VALUE_HEADS), 1)
    two_ranks = 2 * ADAPTER_RANK
    hbm = pl.BlockSpec(memory_space=pl.ANY)
    vmem = pl.BlockSpec(memory_space=pltpu.VMEM)
    smem = pl.BlockSpec(memory_space=pltpu.SMEM)
    dma = pltpu.SemaphoreType.DMA
    results = pl.pallas_call(
        functools.partial(project_kernel, n, stores, chunks, slots),
        in_specs=[hbm] * 6 + [smem, smem, vmem],
        out_specs=[hbm] * 4,
        out_shape=[
            jax.ShapeDtypeStruct((total, query_width), jnp.bfloat16),
            jax.ShapeDtypeStruct((stores, two_ranks, query_width), jnp.bfloat16),
            jax.ShapeDtypeStruct((stores, ADAPTER_RANK, query_width), jnp.bfloat16),
            jax.ShapeDtypeStruct((stores, ADAPTER_RANK, keyval_width), jnp.bfloat16),
        ],
        scratch_shapes=[
            pltpu.VMEM((chunks, total, width), jnp.bfloat16),
            pltpu.VMEM((model_width, query_width), jnp.bfloat16),
            pltpu.VMEM((model_width, keyval_width), jnp.bfloat16),
            pltpu.VMEM((total, query_width), jnp.float32),
            pltpu.VMEM((total, keyval_width), jnp.float32),
            pltpu.VMEM((stores, two_ranks, model_width // n), jnp.bfloat16),
            pltpu.VMEM((stores * ADAPTER_RANK, query_width), jnp.bfloat16),
            pltpu.VMEM((stores * ADAPTER_RANK, keyval_width), jnp.bfloat16),
            pltpu.VMEM((total, two_ranks), jnp.bfloat16),
            pltpu.VMEM((total, two_ranks), jnp.float32),
            pltpu.VMEM((n, 2 * rows, two_ranks), jnp.bfloat16),
            pltpu.VMEM((total, two_ranks), jnp.bfloat16),
            pltpu.VMEM((pair_heads, total, HEAD_SIZE), jnp.bfloat16),
            pltpu.VMEM((kv_used, total, HEAD_SIZE), jnp.bfloat16),
            pltpu.VMEM((kv_used, total, HEAD_SIZE), jnp.bfloat16),
            pltpu.VMEM((kv_used, total, 2 * HEAD_SIZE), jnp.bfloat16),
            pltpu.VMEM((total, total), jnp.float32),
            pltpu.VMEM((total, HEAD_SIZE), jnp.float32),
            pltpu.VMEM((total, HEAD_SIZE), jnp.float32),
            pltpu.VMEM((total, 1), jnp.float32),
            dma((chunks,)),
            dma((2, chunks)),
            dma((2, n, chunks)),
            dma((2, n, chunks)),
            dma((3, stores)),
            dma((3, stores)),
            dma((3,)),
            dma((3, slots)),
            dma((3, stores)),
            dma((n,)),
            dma((n,)),
            dma((n,)),
            dma((n,)),
            dma((2, 2)),
            dma((2, query_width // HEAD_SIZE)),
        ],
        compiler_params=pltpu.CompilerParams(
            collective_id=0, has_side_effects=True, vmem_limit_bytes=67043328
        ),
        name="project",
    )(
        tokens,
        query_weight,
        key_value_weight,
        adapter_down_maps,
        adapter_up_query,
        adapter_up_key_value,
        adapter_row_table,
        request_adapter_ids,
        token_request_ids,
    )
    return hand_over(results[0])


def hand_over_kernel(pieces, source, out, held, in_sem, out_sem):
    count = held.shape[0] // pieces

    def load(k):
        at = pl.ds(k * count, count)
        return pltpu.make_async_copy(source.at[at, :], held.at[at, :], in_sem.at[k])

    def store(k):
        at = pl.ds(k * count, count)
        return pltpu.make_async_copy(held.at[at, :], out.at[at, :], out_sem.at[k])

    for k in range(pieces):
        load(k).start()
    for k in range(pieces):
        load(k).wait()
        store(k).start()
    for k in range(pieces):
        store(k).wait()


def hand_over(attention):
    hbm = pl.BlockSpec(memory_space=pl.ANY)
    pieces = 8
    return pl.pallas_call(
        functools.partial(hand_over_kernel, pieces),
        in_specs=[hbm],
        out_specs=hbm,
        out_shape=jax.ShapeDtypeStruct(attention.shape, attention.dtype),
        scratch_shapes=[
            pltpu.VMEM(attention.shape, attention.dtype),
            pltpu.SemaphoreType.DMA((pieces,)),
            pltpu.SemaphoreType.DMA((pieces,)),
        ],
        name="hand_over",
    )(attention)


def solution(mesh):
    return jax.shard_map(
        on_device,
        mesh=mesh,
        in_specs=(
            P(("groups", "store", "tensor"), None),
            P(None, "tensor"),
            P(None, "tensor"),
            P("store", None, "tensor"),
            P("store", None, "tensor"),
            P("store", None, "tensor"),
            P("groups"),
            P("groups", None),
            P(("groups", "store"), None),
        ),
        out_specs=P(("groups", "store"), "tensor"),
        check_vma=False,
    )
```

```python
import functools
import math

import jax
import jax.numpy as jnp
from jax import lax
from jax.experimental import pallas as pl
from jax.experimental.pallas import tpu as pltpu
from jax.sharding import PartitionSpec as P

MODEL_WIDTH = 8192
QUERY_HEADS = 64
KEY_VALUE_HEADS = 8
HEAD_SIZE = 128
ADAPTER_RANK = 64
STORE_REQUESTS = 4
TOK_ST = 512


adapter_scale = 2.0
rope_theta = 500000.0


MAX_RUN = 256
MESH = pl.DeviceIdType.MESH


def project_kernel(
    n,
    stores,
    chunks,
    slots,
    tokens_ref,
    wq_hbm,
    wkv_hbm,
    down_hbm,
    upq_hbm,
    upkv_hbm,
    table_ref,
    request_ref,
    segment_ref,
    out_ref,
    down_picked,
    upq_picked,
    upkv_picked,
    xbuf,
    wq,
    wkv,
    acc_q,
    acc_kv,
    down,
    upq,
    upkv,
    low_part,
    low_own,
    low_got,
    low_all,
    kv_heads,
    kv_got,
    keys_ref,
    values_ref,
    bias_ref,
    cos_ref,
    sin_ref,
    holder_ref,
    token_sem,
    weight_sem,
    recv_sem,
    send_sem,
    adapter_send,
    adapter_recv,
    adapter_own,
    candidate_sem,
    picked_sem,
    part_send,
    part_recv,
    low_send,
    low_recv,
    kv_sem,
    half_sem,
    out_sem,
):
    t = lax.axis_index("tensor")
    s = lax.axis_index("store")
    rows = tokens_ref.shape[0]
    width = tokens_ref.shape[1] // chunks
    total = rows * n
    query_width = wq.shape[1]
    keyval_width = wkv.shape[1]
    pair_heads = keyval_width // HEAD_SIZE
    head_local = query_width // HEAD_SIZE
    group_size = QUERY_HEADS // KEY_VALUE_HEADS
    kv_used = max(head_local // group_size, 1)

    def kv_first(rank):
        return rank * head_local // group_size - rank // 2 * pair_heads

    barrier = pltpu.get_barrier_semaphore()
    pairs = n // 2
    owners = [2 * m + 1 if 2 * m + 1 < n - 2 * m - 1 else 2 * m for m in range(pairs)]

    def owns(rank):
        m = rank // 2
        return rank == 2 * m + jnp.where(2 * m + 1 < n - 2 * m - 1, 1, 0)

    is_owner = owns(t)
    greeted = 0
    for d in range(1, n):
        peer = lax.rem(t + d, n)
        near = jnp.logical_or(peer == t + 1, peer == t - 1)
        meets = jnp.logical_or(near, jnp.logical_or(is_owner, owns(peer)))
        greeted += jnp.where(meets, 1, 0)

        @pl.when(meets)
        def _():
            pl.semaphore_signal(
                barrier, inc=1, device_id={"tensor": peer}, device_id_type=MESH
            )

    for d in range(1, stores):
        pl.semaphore_signal(
            barrier, inc=1, device_id={"store": lax.rem(s + d, stores)}, device_id_type=MESH
        )

    def own_copy(c):
        return pltpu.make_async_copy(
            tokens_ref.at[:, pl.ds(c * width, width)],
            xbuf.at[c, pl.ds(t * rows, rows), :],
            token_sem.at[c],
        )

    def weight_copies(c):
        part = pl.ds(c * width, width)
        return (
            pltpu.make_async_copy(wq_hbm.at[part, :], wq.at[part, :], weight_sem.at[0, c]),
            pltpu.make_async_copy(wkv_hbm.at[part, :], wkv.at[part, :], weight_sem.at[1, c]),
        )

    model_width = wq.shape[0]
    two_ranks = 2 * ADAPTER_RANK
    picked_down = chunks // 2 * width
    picked_up = picked_down + stores * two_ranks
    picked_end = picked_up + stores * ADAPTER_RANK
    candidate_sets = (
        (down_hbm, wq, 0, two_ranks, picked_down, down_picked),
        (upq_hbm, wq, slots * two_ranks, ADAPTER_RANK, picked_up, upq_picked),
        (upkv_hbm, wkv, 0, ADAPTER_RANK, picked_up, upkv_picked),
    )
    candidates = [
        pltpu.make_async_copy(
            source.at[k], held.at[pl.ds(first + k * count, count), :], candidate_sem.at[j, k]
        )
        for j, (source, held, first, count, _, _) in enumerate(candidate_sets)
        for k in range(slots)
    ]
    adapter_pairs = ((down_picked, down), (upq_picked, upq), (upkv_picked, upkv))

    def adapter_block(held, i, at):
        if i == 0:
            return held.at[at]
        return held.at[pl.ds(at * ADAPTER_RANK, ADAPTER_RANK), :]

    own_adapters = [
        pltpu.make_async_copy(source.at[s], adapter_block(held, i, s), adapter_own.at[i])
        for i, (source, held) in enumerate(adapter_pairs)
    ]

    pl.semaphore_wait(barrier, greeted + stores - 1)

    def place(side, i):
        return chunks - 1 - i if side == 0 else i

    def stream_copy(side, p, i, own):
        c = place(side, i)
        shard = t - p if side == 0 else t + p
        held = xbuf.at[c, pl.ds(shard * rows, rows), :]
        source = tokens_ref.at[:, pl.ds(c * width, width)] if own else held
        return pltpu.make_async_remote_copy(
            src_ref=source,
            dst_ref=held,
            send_sem=send_sem.at[side, p, i],
            recv_sem=recv_sem.at[side, p, i],
            device_id={"tensor": t + 1 if side == 0 else t - 1},
            device_id_type=MESH,
        )

    def arrival(side, p, i):
        c = place(side, i)
        shard = t - p if side == 0 else t + p
        held = xbuf.at[c, pl.ds(shard * rows, rows), :]
        return pltpu.make_async_remote_copy(
            src_ref=held,
            dst_ref=held,
            send_sem=send_sem.at[side, p - 1, i],
            recv_sem=recv_sem.at[side, p - 1, i],
            device_id={"tensor": t - 1 if side == 0 else t + 1},
            device_id_type=MESH,
        )

    is_end = jnp.logical_or(t == 0, t == n - 1)
    share = chunks // n
    can_send = (t < n - 1, t > 0)
    reach = (t, n - 1 - t)

    def item(shards, j):
        head = share * shards
        rest = chunks - share
        in_head = j < head
        k = jnp.maximum(j - head, 0)
        return (
            jnp.where(in_head, j // share, k // rest) + 1,
            jnp.where(in_head, j % share, share + k % rest),
        )

    def send_item(side, j, own):
        p, i = item(reach[side] + 1, j)
        return stream_copy(side, p - 1, i, own)

    half = width // 2
    last_chunk = jnp.where(t >= n - t, 0, chunks - 1)
    last_shard = jnp.where(t >= n - t, 0, n - 1)
    outward = jnp.where(t >= n - t, t + 1, t - 1)

    def half_copy(h):
        held = xbuf.at[
            last_chunk,
            pl.ds(pl.multiple_of(last_shard * rows, rows), rows),
            pl.ds(h * half, half),
        ]
        return pltpu.make_async_remote_copy(
            src_ref=held,
            dst_ref=held,
            send_sem=half_sem.at[0, h],
            recv_sem=half_sem.at[1, h],
            device_id={"tensor": jnp.where(is_end, t + 1 - 2 * (t % 2), outward)},
            device_id_type=MESH,
        )

    def start_send(side, j):
        p, i = item(reach[side] + 1, j)
        is_last = jnp.logical_and(p == n - 1, i == chunks - 1)

        @pl.when(is_last)
        def _():
            for h in range(2):
                half_copy(h).start()

        @pl.when(p == 1)
        def _():
            stream_copy(side, 0, i, True).start()

        @pl.when(jnp.logical_and(p > 1, jnp.logical_not(is_last)))
        def _():
            stream_copy(side, p - 1, i, False).start()

    ahead = 2
    depth = 4
    for j in range(ahead):
        for side in range(2):

            @pl.when(can_send[side])
            def _():
                stream_copy(side, 0, j, True).start()

    for copy in candidates:
        copy.start()
    for c in range(chunks):
        own_copy(c).start()

    tile_q = min(query_width, 512)

    def keyval_unit(c, shard):
        at = pl.ds(pl.multiple_of(shard * rows, rows), rows)
        part = pl.ds(pl.multiple_of(c * width, width), width)
        acc_kv[at, :] += jnp.dot(
            xbuf[c, at, :], wkv[part, :], preferred_element_type=jnp.float32
        )

    def query_unit(c, shard):
        at = pl.ds(pl.multiple_of(shard * rows, rows), rows)
        part = pl.ds(pl.multiple_of(c * width, width), width)

        @pl.loop(0, query_width // tile_q)
        def _(k):
            columns = pl.ds(pl.multiple_of(k * tile_q, tile_q), tile_q)
            acc_q[at, columns] += jnp.dot(
                xbuf[c, at, :], wq[part, columns], preferred_element_type=jnp.float32
            )

    acc_q[...] = jnp.zeros_like(acc_q)
    acc_kv[...] = jnp.zeros_like(acc_kv)
    holds_keys = t % 2 == 0

    def request_column():
        place_row = lax.broadcasted_iota(jnp.int32, (total, total), 0)
        place_column = lax.broadcasted_iota(jnp.int32, (total, total), 1)
        across = segment_ref[...].astype(jnp.float32)
        own = jnp.where(place_row == place_column, across, 0.0)
        return across, jnp.sum(own, axis=1, keepdims=True), place_row >= place_column

    def fill_tables():
        across, down_column, ordered = request_column()
        allowed = jnp.logical_and(down_column == across, ordered)
        bias_ref[...] = jnp.where(allowed, 0.0, -1e30)
        first_index = jnp.sum(jnp.where(across < down_column, 1.0, 0.0), axis=1, keepdims=True)
        place_token = lax.broadcasted_iota(jnp.int32, (total, 1), 0).astype(jnp.float32)
        lane = lax.broadcasted_iota(jnp.int32, (total, HEAD_SIZE), 1)
        exponent = lax.rem(lane, HEAD_SIZE // 2).astype(jnp.float32) * (2.0 / HEAD_SIZE)
        angles = (place_token - first_index) * jnp.exp(-exponent * math.log(rope_theta))
        sine = jnp.sin(angles)
        cos_ref[...] = jnp.cos(angles)
        sin_ref[...] = jnp.where(lane < HEAD_SIZE // 2, -sine, sine)

    def fill_holder():
        _, down_column, _ = request_column()
        holder = jnp.zeros((total, 1), jnp.float32)
        for k in range(STORE_REQUESTS):
            owner = lax.div(table_ref[request_ref[s, k]], slots).astype(jnp.float32)
            holder += jnp.where(down_column == float(k), owner, 0.0)
        holder_ref[...] = holder

    for copy in candidates:
        copy.wait()
    bits = []
    for i in range(stores):
        index = 0
        for k in range(STORE_REQUESTS):
            slot = table_ref[request_ref[i, k]]
            index += jnp.where(lax.div(slot, slots) == s, lax.rem(slot, slots), 0)
        bits.append([lax.rem(lax.div(index, 1 << k), 2) == 1 for k in range(slots.bit_length())])

    def pick(held, first, count, to):
        lanes = min(held.shape[1], 512)

        @pl.loop(0, count // 16)
        def _(r):
            for at in range(0, held.shape[1], lanes):
                columns = slice(at, at + lanes)

                def tile(base, k):
                    return pl.ds(pl.multiple_of(base + k * count + r * 16, 16), 16)

                found = [held[tile(first, k), columns] for k in range(slots)]
                for i in range(stores):
                    left, level = found, 0
                    while len(left) > 1:
                        bit = bits[i][level]
                        left = [
                            jnp.where(bit, left[k + 1], left[k]) if k + 1 < len(left) else left[k]
                            for k in range(0, len(left), 2)
                        ]
                        level += 1
                    held[tile(to, i), columns] = left[0]

    for _, held, first, count, to, _ in candidate_sets:
        pick(held, first, count, to)
    picked_copies = [
        pltpu.make_async_copy(
            held.at[pl.ds(to + i * count, count), :], picked.at[i], picked_sem.at[j, i]
        )
        for j, (_, held, _, count, to, picked) in enumerate(candidate_sets)
        for i in range(stores)
    ]
    for copy in picked_copies:
        copy.start()
    def start_weights(k):
        for c in (k, chunks - 1 - k):
            for copy in weight_copies(c):
                copy.start()

    start_weights(0)
    for copy in picked_copies:
        copy.wait()
    for copy in own_adapters:
        copy.start()
    adapter_sends = []
    for d in range(1, stores):
        for i, (source, held) in enumerate(adapter_pairs):
            peer = lax.rem(s + d, stores)
            copy = pltpu.make_async_remote_copy(
                src_ref=source.at[peer],
                dst_ref=adapter_block(held, i, s),
                send_sem=adapter_send.at[i, d],
                recv_sem=adapter_recv.at[i, d],
                device_id={"store": peer},
                device_id_type=MESH,
            )
            copy.start()
            adapter_sends.append(copy)


    def mask_of(p):
        return jnp.where(holder_ref[...] == float(p), 1.0, 0.0)

    for copy in own_adapters:
        copy.wait()
    for c in range(chunks):
        own_copy(c).wait()

    def low_ready(side):
        first = share * (t if side == 1 else n - 1 - t)
        i = first + share - 1
        shards = reach[side]
        in_rest = share * shards + (shards - 1) * (chunks - share) + i - share
        return jnp.where(shards == 0, 0, jnp.where(i < share, share * shards - 1, in_rest))

    last_step = (n - 1) * chunks - 1
    inner_done = (n - 2) * chunks - 1
    third_at = jnp.where(is_end, last_step - 4, inner_done + 1)
    early_at = last_step - jnp.where(is_end, 4, 3)
    low_at = jnp.maximum(jnp.maximum(low_ready(0), low_ready(1)), chunks)

    own_pair = t // 2

    def pair_rows(m):
        start = m * 2 * rows
        return pl.ds(start if isinstance(m, int) else pl.multiple_of(start, 2 * rows), 2 * rows)

    def part_copy(m):
        return pltpu.make_async_remote_copy(
            src_ref=low_part.at[pair_rows(m), :],
            dst_ref=low_got.at[t],
            send_sem=part_send.at[m],
            recv_sem=part_recv.at[t],
            device_id={"tensor": owners[m]},
            device_id_type=MESH,
        )

    def part_arrival(d):
        source = lax.rem(t + n - d, n)
        return pltpu.make_async_remote_copy(
            src_ref=low_got.at[source],
            dst_ref=low_got.at[source],
            send_sem=part_send.at[0],
            recv_sem=part_recv.at[source],
            device_id={"tensor": source},
            device_id_type=MESH,
        )

    def low_copy(d):
        held = low_all.at[pair_rows(own_pair), :]
        return pltpu.make_async_remote_copy(
            src_ref=held,
            dst_ref=held,
            send_sem=low_send.at[d],
            recv_sem=low_recv.at[own_pair],
            device_id={"tensor": lax.rem(t + d, n)},
            device_id_type=MESH,
        )

    def low_arrival(m):
        held = low_all.at[pair_rows(m), :]
        return pltpu.make_async_remote_copy(
            src_ref=held,
            dst_ref=held,
            send_sem=low_send.at[0],
            recv_sem=low_recv.at[m],
            device_id={"tensor": owners[m]},
            device_id_type=MESH,
        )

    def adapters_arrive():
        for d in range(1, stores):
            source = lax.rem(s + stores - d, stores)
            for i, (_, held) in enumerate(adapter_pairs):
                block = adapter_block(held, i, source)
                pltpu.make_async_remote_copy(
                    src_ref=block,
                    dst_ref=block,
                    send_sem=adapter_send.at[i, d],
                    recv_sem=adapter_recv.at[i, d],
                    device_id={"store": source},
                    device_id_type=MESH,
                ).wait_recv()

    def low_first():
        fill_holder()
        adapters_arrive()
        summed = jnp.zeros(low_part.shape, jnp.float32)
        for p in range(stores):
            picked = jnp.zeros(low_part.shape, jnp.float32)
            for k in range(share):
                picked += lax.dot_general(
                    xbuf[t * share + k],
                    down[p, :, k * width : (k + 1) * width],
                    (((1,), (1,)), ((), ())),
                    preferred_element_type=jnp.float32,
                )
            summed += picked * mask_of(p)
        low_part[...] = summed.astype(jnp.bfloat16)
        low_own[...] = summed
        for m in range(pairs):

            @pl.when(t != owners[m])
            def _():
                part_copy(m).start()

    def low_second():
        at = pair_rows(own_pair)
        whole = low_own[at, :]
        for d in range(1, n):
            part_arrival(d).wait_recv()
            whole += low_got[lax.rem(t + n - d, n)].astype(jnp.float32)
        low_all[at, :] = whole.astype(jnp.bfloat16)
        for d in range(1, n):
            low_copy(d).start()

    def spread_low(lower):
        low = low_all[...].astype(jnp.float32)
        turned = pltpu.roll(low, ADAPTER_RANK, 1)
        in_lower = lax.broadcasted_iota(jnp.int32, low.shape, 1) < ADAPTER_RANK
        twice = jnp.where(in_lower, low, turned) if lower else jnp.where(in_lower, turned, low)
        masks = [
            jnp.where(in_lower, mask_of(2 * p), mask_of(2 * p + 1)) for p in range(stores // 2)
        ]
        return jnp.concatenate([(twice * m).astype(jnp.bfloat16) for m in masks], axis=1)

    def low_keyval():
        for m in range(pairs):

            @pl.when(t != owners[m])
            def _():
                low_arrival(m).wait_recv()

        acc_kv[...] += adapter_scale * jnp.dot(
            spread_low(False), upkv[...], preferred_element_type=jnp.float32
        )

    def low_query():
        spread = spread_low(True)
        for k in range(query_width // tile_q):
            columns = slice(k * tile_q, (k + 1) * tile_q)
            acc_q[:, columns] += adapter_scale * jnp.dot(
                spread, upq[:, columns], preferred_element_type=jnp.float32
            )

    def rotated(value, cosine, sine):
        return value * cosine + pltpu.roll(value, HEAD_SIZE // 2, 1) * sine

    ends_first = t >= n - t
    early_start = pl.multiple_of(jnp.where(ends_first, rows, 0), rows)
    late_start = pl.multiple_of(jnp.where(ends_first, 0, total - rows), rows)
    partner = t + 1 - 2 * (t % 2)

    def finish_keyval(start, count):
        at = pl.ds(start, count)
        cosine = jnp.where(holds_keys, cos_ref[at, :], 1.0)
        sine = jnp.where(holds_keys, sin_ref[at, :], 0.0)
        for m in range(pair_heads):
            value = acc_kv[at, m * HEAD_SIZE : (m + 1) * HEAD_SIZE]
            kv_heads[m, at, :] = rotated(value, cosine, sine).astype(jnp.bfloat16)

    def keyval_copy(start, count, which):
        at = pl.ds(start, count)
        return pltpu.make_async_remote_copy(
            src_ref=kv_heads.at[pl.ds(kv_first(partner), kv_used), at, :],
            dst_ref=kv_got.at[:, at, :],
            send_sem=kv_sem.at[0, which],
            recv_sem=kv_sem.at[1, which],
            device_id={"tensor": partner},
            device_id_type=MESH,
        )

    own_first = kv_first(t)
    is_inner = jnp.logical_not(is_end)
    starts_first = jnp.logical_not(ends_first)
    holds_values = jnp.logical_not(holds_keys)
    early_count = total - rows
    per_kv = head_local // kv_used
    batch = min(8, per_kv)
    block = 128
    blocks = total // block
    scale = 1.0 / math.sqrt(HEAD_SIZE) / math.log(2.0)
    stage_at = pl.multiple_of(jnp.where(ends_first, model_width - total, 0), total)
    part_at = pl.multiple_of(jnp.where(ends_first, model_width - 2 * total, total), total)

    def finish_late():
        finish_keyval(late_start, rows)
        keyval_copy(late_start, rows, 1).start()

    def gather_keys(start, count):
        at = pl.ds(start, count)
        for g in range(kv_used):

            @pl.when(holds_keys)
            def _():
                keys_ref[g, at, :] = kv_heads[own_first + g, at, :]

            @pl.when(holds_values)
            def _():
                keys_ref[g, at, :] = kv_got[g, at, :]

    def gather_values(start, count):
        at = pl.ds(start, count)
        for g in range(kv_used):

            @pl.when(holds_keys)
            def _():
                values_ref[g, at, :HEAD_SIZE] = kv_got[g, at, :]

            @pl.when(holds_values)
            def _():
                values_ref[g, at, :HEAD_SIZE] = kv_heads[own_first + g, at, :]

    def lanes_of(h):
        return pl.ds(pl.multiple_of(h * HEAD_SIZE, HEAD_SIZE), HEAD_SIZE)

    def stage_rows(start, first, count):
        return pl.ds(pl.multiple_of(start + first, block), count)

    def scores_of(b, g, lanes, low, high):
        at = slice(b * block, (b + 1) * block)
        query = [
            rotated(acc_q[at, ln], cos_ref[at, :], sin_ref[at, :]).astype(jnp.bfloat16)
            for ln in lanes
        ]
        scores = lax.dot_general(
            jnp.concatenate(query, axis=0),
            keys_ref[g, low:high, :],
            (((1,), (1,)), ((), ())),
            preferred_element_type=jnp.float32,
        )
        scores = scores.reshape(2, block, high - low) + bias_ref[at, low:high][None]
        return scores.reshape(2 * block, high - low)

    def weights_of(b, g, lanes):
        scores = scores_of(b, g, lanes, max(0, b * block - MAX_RUN), (b + 1) * block)
        scores = (scores - jnp.max(scores, axis=1, keepdims=True)) * scale
        return jnp.exp2(scores).astype(jnp.bfloat16)

    def attend(b, g, lanes):
        low = max(0, b * block - MAX_RUN)
        high = (b + 1) * block
        mixed = jnp.dot(
            weights_of(b, g, lanes), values_ref[g, low:high, :], preferred_element_type=jnp.float32
        )
        mixed = (mixed[:, :HEAD_SIZE] / mixed[:, HEAD_SIZE:]).astype(jnp.bfloat16)
        for k, ln in enumerate(lanes):
            wq[stage_rows(stage_at, b * block, block), ln] = mixed[k * block : (k + 1) * block]

    def attend_part(b, g, lanes):
        high = (b + 1) * block
        weights = weights_of(b, g, lanes)
        first = weights[:, :block]
        sums = jnp.dot(
            first, values_ref[g, :block, HEAD_SIZE:], preferred_element_type=jnp.float32
        )
        if b > 0:
            mixed = jnp.dot(
                weights[:, block:], values_ref[g, block:high, :], preferred_element_type=jnp.float32
            )
            sums += mixed[:, HEAD_SIZE:]
        inverse = 1.0 / sums
        rest = mixed[:, :HEAD_SIZE] * inverse if b > 0 else jnp.zeros_like(inverse)
        first = (first.astype(jnp.float32) * inverse).astype(jnp.bfloat16)
        for k, ln in enumerate(lanes):
            acc_q[b * block : high, ln] = rest[k * block : (k + 1) * block]
            wq[stage_rows(part_at, b * block, block), ln] = first[k * block : (k + 1) * block]

    def attend_rest(b, g, ln):
        first, count = b * block, (blocks - 1 - b) * block
        more = jnp.dot(
            wq[stage_rows(part_at, first, count), ln],
            values_ref[g, :block, :HEAD_SIZE],
            preferred_element_type=jnp.float32,
        )
        whole = acc_q[first : first + count, ln] + more
        wq[stage_rows(stage_at, first, count), ln] = whole.astype(jnp.bfloat16)

    last = (blocks - 1) * block
    kept = [slice(k * block, (k + 1) * block) for k in range(3)]

    def attend_start(g, lanes):
        scores = scores_of(blocks - 1, g, lanes, last - MAX_RUN, last)
        top = jnp.max(scores, axis=1, keepdims=True)
        weights = jnp.exp2((scores - top) * scale).astype(jnp.bfloat16)
        mixed = jnp.dot(
            weights, values_ref[g, last - MAX_RUN : last, :], preferred_element_type=jnp.float32
        )
        for k, ln in enumerate(lanes):
            at = slice(k * block, (k + 1) * block)
            acc_q[kept[0], ln] = mixed[at, :HEAD_SIZE]
            acc_q[kept[1], ln] = mixed[at, HEAD_SIZE:]
            acc_q[kept[2], ln] = jnp.broadcast_to(top[at], (block, HEAD_SIZE))

    def attend_finish(g, lanes):
        scores = scores_of(blocks - 1, g, lanes, last, total)
        total_of, sum_of, top_of = (
            jnp.concatenate([acc_q[at, ln] for ln in lanes], axis=0) for at in kept
        )
        top = jnp.maximum(top_of, jnp.max(scores, axis=1, keepdims=True))
        weights = jnp.exp2((scores - top) * scale).astype(jnp.bfloat16)
        shrink = jnp.exp2((top_of - top) * scale)
        mixed = jnp.dot(
            weights, values_ref[g, last:total, :], preferred_element_type=jnp.float32
        )
        sums = sum_of * shrink + mixed[:, HEAD_SIZE:]
        mixed = ((total_of * shrink + mixed[:, :HEAD_SIZE]) / sums).astype(jnp.bfloat16)
        for k, ln in enumerate(lanes):
            wq[stage_rows(stage_at, last, block), ln] = mixed[k * block : (k + 1) * block]

    cut = total - block

    def out_copy(q, which):
        first, count = (0, cut) if which == 0 else (cut, block)
        lanes = pl.ds(pl.multiple_of(q * batch * HEAD_SIZE, batch * HEAD_SIZE), batch * HEAD_SIZE)
        return pltpu.make_async_copy(
            wq.at[stage_rows(stage_at, first, count), lanes],
            out_ref.at[pl.ds(first, count), lanes],
            out_sem.at[which, q],
        )

    def heads(body, which, q):
        g = q * batch // per_kv
        for pair in range(batch // 2):
            body(g, [lanes_of(q * batch + 2 * pair + k) for k in range(2)])
        out_copy(q, which).start()

    def over_heads(body, which):
        @pl.loop(0, head_local // batch)
        def _(q):
            heads(body, which, q)

    def early_keyval():
        keyval_copy(early_start, early_count, 0).wait_recv()
        gather_keys(early_start, early_count)
        gather_values(early_start, early_count)

        @pl.when(ends_first)
        def _():
            @pl.when(holds_values)
            def _():
                keyval_copy(late_start, rows, 1).wait_recv()

            gather_keys(late_start, rows)

    def early_attention(q):
        def lower(inner):
            def body(g, lanes):
                for b in range(blocks - 1):
                    attend(b, g, lanes)
                if inner:
                    attend_start(g, lanes)

            return body

        def upper(inner):
            def body(g, lanes):
                attend(blocks - 1, g, lanes)
                for b in range(0 if inner else 1, blocks - 1):
                    attend_part(b, g, lanes)

            return body

        for inner, where in ((False, is_end), (True, is_inner)):

            @pl.when(jnp.logical_and(where, starts_first))
            def _():
                heads(lower(inner), 0, q)

            @pl.when(jnp.logical_and(where, ends_first))
            def _():
                heads(upper(inner), 1, q)

    def late_attention():
        def lower(inner):
            def body(g, lanes):
                if inner:
                    attend_finish(g, lanes)
                else:
                    attend(blocks - 1, g, lanes)

            return body

        def upper(inner):
            def body(g, lanes):
                if not inner:
                    attend(0, g, lanes)
                for ln in lanes:
                    attend_rest(0 if inner else 1, g, ln)

            return body

        @pl.when(starts_first)
        def _():
            keyval_copy(late_start, rows, 1).wait_recv()
            gather_keys(late_start, rows)
            gather_values(late_start, rows)

        @pl.when(ends_first)
        def _():
            @pl.when(holds_keys)
            def _():
                keyval_copy(late_start, rows, 1).wait_recv()

            gather_values(late_start, rows)

        for inner, where in ((False, is_end), (True, is_inner)):

            @pl.when(jnp.logical_and(where, starts_first))
            def _():
                over_heads(lower(inner), 1)

            @pl.when(jnp.logical_and(where, ends_first))
            def _():
                over_heads(upper(inner), 0)

    for g in range(kv_used):
        values_ref[g, :, HEAD_SIZE:] = jnp.ones((total, HEAD_SIZE), jnp.bfloat16)

    @pl.loop(0, last_step)
    def _(step):
        here = tuple(step < reach[side] * chunks for side in range(2))
        places = [item(reach[side], step) for side in range(2)]
        for side in range(2):
            p, i = places[side]

            @pl.when(here[side])
            def _():
                arrival(side, p, i).wait_recv()

            sends = (reach[side] + 1) * chunks
            head = (reach[side] + 1) * share

            @pl.when(jnp.logical_and(can_send[side], step + depth - 1 < sends))
            def _():
                send_item(side, step, False).wait_send()

                @pl.when(step + ahead <= head)
                def _():
                    start_send(side, step + ahead)

                @pl.when(step + ahead == head)
                def _():
                    for j in range(1, depth - 1):
                        start_send(side, step + ahead + j)

                nearer = step > inner_done
                later = step + depth - jnp.where(nearer, 1, 0)
                wanted = jnp.logical_and(step + ahead > head, step != inner_done + 1)

                @pl.when(jnp.logical_and(wanted, later < sends))
                def _():
                    start_send(side, later)

        @pl.when(step < chunks // 2)
        def _():
            for c in (step, chunks - 1 - step):
                for copy in weight_copies(c):
                    copy.wait()

            @pl.when(step + 1 < chunks // 2)
            def _():
                start_weights(step + 1)

        for side in range(2):
            p, i = places[side]

            @pl.when(here[side])
            def _():
                keyval_unit(place(side, i), t - p if side == 0 else t + p)

        for side in range(2):
            p, i = places[side]

            @pl.when(here[side])
            def _():
                query_unit(place(side, i), t - p if side == 0 else t + p)

        @pl.when(jnp.logical_and(step >= chunks, step < 2 * chunks))
        def _():
            keyval_unit(step - chunks, t)
            query_unit(step - chunks, t)

        @pl.when(step == chunks - 2)
        def _():
            fill_tables()

        @pl.when(step == low_at)
        def _():
            low_first()

        @pl.when(jnp.logical_and(is_owner, step == inner_done))
        def _():
            low_second()

        @pl.when(step == third_at)
        def _():
            low_keyval()
            finish_keyval(early_start, early_count)
            keyval_copy(early_start, early_count, 0).start()

            @pl.when(is_inner)
            def _():
                finish_late()

            low_query()

        @pl.when(step == early_at)
        def _():
            early_keyval()

        @pl.when(jnp.logical_and(step >= early_at, step < early_at + head_local // batch))
        def _():
            early_attention(step - early_at)

    @pl.when(is_end)
    def _():
        at = pl.ds(late_start, rows)
        for h in range(2):
            half_copy(h).wait_recv()
            part = pl.ds(pl.multiple_of(last_chunk * width + h * half, half), half)
            x = xbuf[last_chunk, at, h * half : (h + 1) * half]
            acc_kv[at, :] += jnp.dot(x, wkv[part, :], preferred_element_type=jnp.float32)
            if h == 1:
                finish_late()

            @pl.loop(0, query_width // tile_q)
            def _(k):
                columns = pl.ds(pl.multiple_of(k * tile_q, tile_q), tile_q)
                acc_q[at, columns] += jnp.dot(
                    xbuf[last_chunk, at, h * half : (h + 1) * half],
                    wq[part, columns],
                    preferred_element_type=jnp.float32,
                )

    late_attention()

    for copy in adapter_sends:
        copy.wait_send()
    for m in range(pairs):

        @pl.when(t != owners[m])
        def _():
            part_copy(m).wait_send()

    @pl.when(is_owner)
    def _():
        for d in range(1, n):
            low_copy(d).wait_send()

    keyval_copy(early_start, early_count, 0).wait_send()
    keyval_copy(late_start, rows, 1).wait_send()

    for side in range(2):

        @pl.when(can_send[side])
        def _():
            for j in range(1, depth - 1):
                send_item(side, (reach[side] + 1) * chunks - depth + j, False).wait_send()

            @pl.when(reach[side] < n - 2)
            def _():
                send_item(side, (reach[side] + 1) * chunks - 1, False).wait_send()

            @pl.when(reach[side] == n - 2)
            def _():
                for h in range(2):
                    half_copy(h).wait_send()

    @pl.loop(0, head_local // batch)
    def _(q):
        for which in range(2):
            out_copy(q, which).wait()


def on_device(
    tokens,
    query_weight,
    key_value_weight,
    adapter_down_maps,
    adapter_up_query,
    adapter_up_key_value,
    adapter_row_table,
    request_adapter_ids,
    token_request_ids,
):
    n = lax.axis_size("tensor")
    stores = lax.axis_size("store")
    slots = adapter_down_maps.shape[0]
    rows, model_width = tokens.shape
    total = rows * n
    query_width = query_weight.shape[1]
    keyval_width = key_value_weight.shape[1]
    chunks = max(8, 2 * n)
    width = model_width // chunks
    pair_heads = keyval_width // HEAD_SIZE
    kv_used = max(query_width // HEAD_SIZE // (QUERY_HEADS // KEY_VALUE_HEADS), 1)
    two_ranks = 2 * ADAPTER_RANK
    hbm = pl.BlockSpec(memory_space=pl.ANY)
    vmem = pl.BlockSpec(memory_space=pltpu.VMEM)
    smem = pl.BlockSpec(memory_space=pltpu.SMEM)
    dma = pltpu.SemaphoreType.DMA
    results = pl.pallas_call(
        functools.partial(project_kernel, n, stores, chunks, slots),
        in_specs=[hbm] * 6 + [smem, smem, vmem],
        out_specs=[hbm] * 4,
        out_shape=[
            jax.ShapeDtypeStruct((total, query_width), jnp.bfloat16),
            jax.ShapeDtypeStruct((stores, two_ranks, query_width), jnp.bfloat16),
            jax.ShapeDtypeStruct((stores, ADAPTER_RANK, query_width), jnp.bfloat16),
            jax.ShapeDtypeStruct((stores, ADAPTER_RANK, keyval_width), jnp.bfloat16),
        ],
        scratch_shapes=[
            pltpu.VMEM((chunks, total, width), jnp.bfloat16),
            pltpu.VMEM((model_width, query_width), jnp.bfloat16),
            pltpu.VMEM((model_width, keyval_width), jnp.bfloat16),
            pltpu.VMEM((total, query_width), jnp.float32),
            pltpu.VMEM((total, keyval_width), jnp.float32),
            pltpu.VMEM((stores, two_ranks, model_width // n), jnp.bfloat16),
            pltpu.VMEM((stores * ADAPTER_RANK, query_width), jnp.bfloat16),
            pltpu.VMEM((stores * ADAPTER_RANK, keyval_width), jnp.bfloat16),
            pltpu.VMEM((total, two_ranks), jnp.bfloat16),
            pltpu.VMEM((total, two_ranks), jnp.float32),
            pltpu.VMEM((n, 2 * rows, two_ranks), jnp.bfloat16),
            pltpu.VMEM((total, two_ranks), jnp.bfloat16),
            pltpu.VMEM((pair_heads, total, HEAD_SIZE), jnp.bfloat16),
            pltpu.VMEM((kv_used, total, HEAD_SIZE), jnp.bfloat16),
            pltpu.VMEM((kv_used, total, HEAD_SIZE), jnp.bfloat16),
            pltpu.VMEM((kv_used, total, 2 * HEAD_SIZE), jnp.bfloat16),
            pltpu.VMEM((total, total), jnp.float32),
            pltpu.VMEM((total, HEAD_SIZE), jnp.float32),
            pltpu.VMEM((total, HEAD_SIZE), jnp.float32),
            pltpu.VMEM((total, 1), jnp.float32),
            dma((chunks,)),
            dma((2, chunks)),
            dma((2, n, chunks)),
            dma((2, n, chunks)),
            dma((3, stores)),
            dma((3, stores)),
            dma((3,)),
            dma((3, slots)),
            dma((3, stores)),
            dma((n,)),
            dma((n,)),
            dma((n,)),
            dma((n,)),
            dma((2, 2)),
            dma((2, 2)),
            dma((2, query_width // HEAD_SIZE)),
        ],
        compiler_params=pltpu.CompilerParams(
            collective_id=0, has_side_effects=True, vmem_limit_bytes=67043328
        ),
        name="project",
    )(
        tokens,
        query_weight,
        key_value_weight,
        adapter_down_maps,
        adapter_up_query,
        adapter_up_key_value,
        adapter_row_table,
        request_adapter_ids,
        token_request_ids,
    )
    return hand_over(results[0])


def hand_over_kernel(pieces, source, out, held, in_sem, out_sem):
    count = held.shape[0] // pieces

    def load(k):
        at = pl.ds(k * count, count)
        return pltpu.make_async_copy(source.at[at, :], held.at[at, :], in_sem.at[k])

    def store(k):
        at = pl.ds(k * count, count)
        return pltpu.make_async_copy(held.at[at, :], out.at[at, :], out_sem.at[k])

    for k in range(pieces):
        load(k).start()
    for k in range(pieces):
        load(k).wait()
        store(k).start()
    for k in range(pieces):
        store(k).wait()


def hand_over(attention):
    hbm = pl.BlockSpec(memory_space=pl.ANY)
    pieces = 8
    return pl.pallas_call(
        functools.partial(hand_over_kernel, pieces),
        in_specs=[hbm],
        out_specs=hbm,
        out_shape=jax.ShapeDtypeStruct(attention.shape, attention.dtype),
        scratch_shapes=[
            pltpu.VMEM(attention.shape, attention.dtype),
            pltpu.SemaphoreType.DMA((pieces,)),
            pltpu.SemaphoreType.DMA((pieces,)),
        ],
        name="hand_over",
    )(attention)


def solution(mesh):
    return jax.shard_map(
        on_device,
        mesh=mesh,
        in_specs=(
            P(("groups", "store", "tensor"), None),
            P(None, "tensor"),
            P(None, "tensor"),
            P("store", None, "tensor"),
            P("store", None, "tensor"),
            P("store", None, "tensor"),
            P("groups"),
            P("groups", None),
            P(("groups", "store"), None),
        ),
        out_specs=P(("groups", "store"), "tensor"),
        check_vma=False,
    )
```

```python
import functools
import math

import jax
import jax.numpy as jnp
from jax import lax
from jax.experimental import pallas as pl
from jax.experimental.pallas import tpu as pltpu
from jax.sharding import PartitionSpec as P

MODEL_WIDTH = 8192
QUERY_HEADS = 64
KEY_VALUE_HEADS = 8
HEAD_SIZE = 128
ADAPTER_RANK = 64
STORE_REQUESTS = 4
TOK_ST = 512


adapter_scale = 2.0
rope_theta = 500000.0


MAX_RUN = 256
MESH = pl.DeviceIdType.MESH


def project_kernel(
    n,
    stores,
    chunks,
    slots,
    tokens_ref,
    wq_hbm,
    wkv_hbm,
    down_hbm,
    upq_hbm,
    upkv_hbm,
    table_ref,
    request_ref,
    segment_ref,
    out_ref,
    down_picked,
    upq_picked,
    upkv_picked,
    xbuf,
    wq,
    wkv,
    acc_q,
    acc_kv,
    down,
    upq,
    upkv,
    low_part,
    low_own,
    low_got,
    low_all,
    kv_heads,
    kv_got,
    keys_ref,
    values_ref,
    twin_ref,
    bias_ref,
    cos_ref,
    sin_ref,
    holder_ref,
    token_sem,
    weight_sem,
    recv_sem,
    send_sem,
    adapter_send,
    adapter_recv,
    adapter_own,
    candidate_sem,
    picked_sem,
    part_send,
    part_recv,
    low_send,
    low_recv,
    kv_sem,
    half_sem,
    out_sem,
):
    t = lax.axis_index("tensor")
    s = lax.axis_index("store")
    rows = tokens_ref.shape[0]
    width = tokens_ref.shape[1] // chunks
    total = rows * n
    query_width = wq.shape[1]
    keyval_width = wkv.shape[1]
    pair_heads = keyval_width // HEAD_SIZE
    head_local = query_width // HEAD_SIZE
    group_size = QUERY_HEADS // KEY_VALUE_HEADS
    kv_used = max(head_local // group_size, 1)

    def kv_first(rank):
        return rank * head_local // group_size - rank // 2 * pair_heads

    barrier = pltpu.get_barrier_semaphore()
    pairs = n // 2
    owners = [2 * m + 1 if 2 * m + 1 < n - 2 * m - 1 else 2 * m for m in range(pairs)]

    def owns(rank):
        m = rank // 2
        return rank == 2 * m + jnp.where(2 * m + 1 < n - 2 * m - 1, 1, 0)

    is_owner = owns(t)
    greeted = 0
    for d in range(1, n):
        peer = lax.rem(t + d, n)
        near = jnp.logical_or(peer == t + 1, peer == t - 1)
        meets = jnp.logical_or(near, jnp.logical_or(is_owner, owns(peer)))
        greeted += jnp.where(meets, 1, 0)

        @pl.when(meets)
        def _():
            pl.semaphore_signal(
                barrier, inc=1, device_id={"tensor": peer}, device_id_type=MESH
            )

    for d in range(1, stores):
        pl.semaphore_signal(
            barrier, inc=1, device_id={"store": lax.rem(s + d, stores)}, device_id_type=MESH
        )

    def own_copy(c):
        return pltpu.make_async_copy(
            tokens_ref.at[:, pl.ds(c * width, width)],
            xbuf.at[c, pl.ds(t * rows, rows), :],
            token_sem.at[c],
        )

    def weight_copies(c):
        part = pl.ds(c * width, width)
        return (
            pltpu.make_async_copy(wq_hbm.at[part, :], wq.at[part, :], weight_sem.at[0, c]),
            pltpu.make_async_copy(wkv_hbm.at[part, :], wkv.at[part, :], weight_sem.at[1, c]),
        )

    model_width = wq.shape[0]
    two_ranks = 2 * ADAPTER_RANK
    picked_down = chunks // 2 * width
    picked_up = picked_down + stores * two_ranks
    picked_end = picked_up + stores * ADAPTER_RANK
    candidate_sets = (
        (down_hbm, wq, 0, two_ranks, picked_down, down_picked),
        (upq_hbm, wq, slots * two_ranks, ADAPTER_RANK, picked_up, upq_picked),
        (upkv_hbm, wkv, 0, ADAPTER_RANK, picked_up, upkv_picked),
    )
    candidates = [
        pltpu.make_async_copy(
            source.at[k], held.at[pl.ds(first + k * count, count), :], candidate_sem.at[j, k]
        )
        for j, (source, held, first, count, _, _) in enumerate(candidate_sets)
        for k in range(slots)
    ]
    adapter_pairs = ((down_picked, down), (upq_picked, upq), (upkv_picked, upkv))

    def adapter_block(held, i, at):
        if i == 0:
            return held.at[at]
        return held.at[pl.ds(at * ADAPTER_RANK, ADAPTER_RANK), :]

    own_adapters = [
        pltpu.make_async_copy(source.at[s], adapter_block(held, i, s), adapter_own.at[i])
        for i, (source, held) in enumerate(adapter_pairs)
    ]

    pl.semaphore_wait(barrier, greeted + stores - 1)

    def place(side, i):
        return chunks - 1 - i if side == 0 else i

    def stream_copy(side, p, i, own):
        c = place(side, i)
        shard = t - p if side == 0 else t + p
        held = xbuf.at[c, pl.ds(shard * rows, rows), :]
        source = tokens_ref.at[:, pl.ds(c * width, width)] if own else held
        return pltpu.make_async_remote_copy(
            src_ref=source,
            dst_ref=held,
            send_sem=send_sem.at[side, p, i],
            recv_sem=recv_sem.at[side, p, i],
            device_id={"tensor": t + 1 if side == 0 else t - 1},
            device_id_type=MESH,
        )

    def arrival(side, p, i):
        c = place(side, i)
        shard = t - p if side == 0 else t + p
        held = xbuf.at[c, pl.ds(shard * rows, rows), :]
        return pltpu.make_async_remote_copy(
            src_ref=held,
            dst_ref=held,
            send_sem=send_sem.at[side, p - 1, i],
            recv_sem=recv_sem.at[side, p - 1, i],
            device_id={"tensor": t - 1 if side == 0 else t + 1},
            device_id_type=MESH,
        )

    is_end = jnp.logical_or(t == 0, t == n - 1)
    share = chunks // n
    can_send = (t < n - 1, t > 0)
    reach = (t, n - 1 - t)

    def item(shards, j):
        head = share * shards
        rest = chunks - share
        in_head = j < head
        k = jnp.maximum(j - head, 0)
        return (
            jnp.where(in_head, j // share, k // rest) + 1,
            jnp.where(in_head, j % share, share + k % rest),
        )

    def send_item(side, j, own):
        p, i = item(reach[side] + 1, j)
        return stream_copy(side, p - 1, i, own)

    half = width // 2
    last_chunk = jnp.where(t >= n - t, 0, chunks - 1)
    last_shard = jnp.where(t >= n - t, 0, n - 1)
    outward = jnp.where(t >= n - t, t + 1, t - 1)

    def half_copy(h):
        held = xbuf.at[
            last_chunk,
            pl.ds(pl.multiple_of(last_shard * rows, rows), rows),
            pl.ds(h * half, half),
        ]
        return pltpu.make_async_remote_copy(
            src_ref=held,
            dst_ref=held,
            send_sem=half_sem.at[0, h],
            recv_sem=half_sem.at[1, h],
            device_id={"tensor": jnp.where(is_end, t + 1 - 2 * (t % 2), outward)},
            device_id_type=MESH,
        )

    def start_send(side, j):
        p, i = item(reach[side] + 1, j)
        is_last = jnp.logical_and(p == n - 1, i == chunks - 1)

        @pl.when(is_last)
        def _():
            for h in range(2):
                half_copy(h).start()

        @pl.when(p == 1)
        def _():
            stream_copy(side, 0, i, True).start()

        @pl.when(jnp.logical_and(p > 1, jnp.logical_not(is_last)))
        def _():
            stream_copy(side, p - 1, i, False).start()

    ahead = 2
    depth = 4
    for j in range(ahead):
        for side in range(2):

            @pl.when(can_send[side])
            def _():
                stream_copy(side, 0, j, True).start()

    for copy in candidates:
        copy.start()
    for c in range(chunks):
        own_copy(c).start()

    tile_q = min(query_width, 512)

    def keyval_unit(c, shard):
        at = pl.ds(pl.multiple_of(shard * rows, rows), rows)
        part = pl.ds(pl.multiple_of(c * width, width), width)
        acc_kv[at, :] += jnp.dot(
            xbuf[c, at, :], wkv[part, :], preferred_element_type=jnp.float32
        )

    def query_unit(c, shard):
        at = pl.ds(pl.multiple_of(shard * rows, rows), rows)
        part = pl.ds(pl.multiple_of(c * width, width), width)

        @pl.loop(0, query_width // tile_q)
        def _(k):
            columns = pl.ds(pl.multiple_of(k * tile_q, tile_q), tile_q)
            acc_q[at, columns] += jnp.dot(
                xbuf[c, at, :], wq[part, columns], preferred_element_type=jnp.float32
            )

    acc_q[...] = jnp.zeros_like(acc_q)
    acc_kv[...] = jnp.zeros_like(acc_kv)
    holds_keys = t % 2 == 0

    def request_column():
        place_row = lax.broadcasted_iota(jnp.int32, (total, total), 0)
        place_column = lax.broadcasted_iota(jnp.int32, (total, total), 1)
        across = segment_ref[...].astype(jnp.float32)
        own = jnp.where(place_row == place_column, across, 0.0)
        return across, jnp.sum(own, axis=1, keepdims=True), place_row >= place_column

    def fill_tables():
        across, down_column, ordered = request_column()
        allowed = jnp.logical_and(down_column == across, ordered)
        bias_ref[...] = jnp.where(allowed, 0.0, -1e30)
        first_index = jnp.sum(jnp.where(across < down_column, 1.0, 0.0), axis=1, keepdims=True)
        place_token = lax.broadcasted_iota(jnp.int32, (total, 1), 0).astype(jnp.float32)
        lane = lax.broadcasted_iota(jnp.int32, (total, HEAD_SIZE), 1)
        exponent = lax.rem(lane, HEAD_SIZE // 2).astype(jnp.float32) * (2.0 / HEAD_SIZE)
        angles = (place_token - first_index) * jnp.exp(-exponent * math.log(rope_theta))
        sine = jnp.sin(angles)
        cos_ref[...] = jnp.cos(angles)
        sin_ref[...] = jnp.where(lane < HEAD_SIZE // 2, -sine, sine)

    def fill_holder():
        _, down_column, _ = request_column()
        holder = jnp.zeros((total, 1), jnp.float32)
        for k in range(STORE_REQUESTS):
            owner = lax.div(table_ref[request_ref[s, k]], slots).astype(jnp.float32)
            holder += jnp.where(down_column == float(k), owner, 0.0)
        holder_ref[...] = holder

    for copy in candidates:
        copy.wait()
    bits = []
    for i in range(stores):
        index = 0
        for k in range(STORE_REQUESTS):
            slot = table_ref[request_ref[i, k]]
            index += jnp.where(lax.div(slot, slots) == s, lax.rem(slot, slots), 0)
        bits.append([lax.rem(lax.div(index, 1 << k), 2) == 1 for k in range(slots.bit_length())])

    def pick(held, first, count, to):
        lanes = min(held.shape[1], 512)

        @pl.loop(0, count // 16)
        def _(r):
            for at in range(0, held.shape[1], lanes):
                columns = slice(at, at + lanes)

                def tile(base, k):
                    return pl.ds(pl.multiple_of(base + k * count + r * 16, 16), 16)

                found = [held[tile(first, k), columns] for k in range(slots)]
                for i in range(stores):
                    left, level = found, 0
                    while len(left) > 1:
                        bit = bits[i][level]
                        left = [
                            jnp.where(bit, left[k + 1], left[k]) if k + 1 < len(left) else left[k]
                            for k in range(0, len(left), 2)
                        ]
                        level += 1
                    held[tile(to, i), columns] = left[0]

    for _, held, first, count, to, _ in candidate_sets:
        pick(held, first, count, to)
    picked_copies = [
        pltpu.make_async_copy(
            held.at[pl.ds(to + i * count, count), :], picked.at[i], picked_sem.at[j, i]
        )
        for j, (_, held, _, count, to, picked) in enumerate(candidate_sets)
        for i in range(stores)
    ]
    for copy in picked_copies:
        copy.start()
    def start_weights(k):
        for c in (k, chunks - 1 - k):
            for copy in weight_copies(c):
                copy.start()

    start_weights(0)
    for copy in picked_copies:
        copy.wait()
    for copy in own_adapters:
        copy.start()
    adapter_sends = []
    for d in range(1, stores):
        for i, (source, held) in enumerate(adapter_pairs):
            peer = lax.rem(s + d, stores)
            copy = pltpu.make_async_remote_copy(
                src_ref=source.at[peer],
                dst_ref=adapter_block(held, i, s),
                send_sem=adapter_send.at[i, d],
                recv_sem=adapter_recv.at[i, d],
                device_id={"store": peer},
                device_id_type=MESH,
            )
            copy.start()
            adapter_sends.append(copy)


    def mask_of(p):
        return jnp.where(holder_ref[...] == float(p), 1.0, 0.0)

    for copy in own_adapters:
        copy.wait()
    for c in range(chunks):
        own_copy(c).wait()

    def low_ready(side):
        first = share * (t if side == 1 else n - 1 - t)
        i = first + share - 1
        shards = reach[side]
        in_rest = share * shards + (shards - 1) * (chunks - share) + i - share
        return jnp.where(shards == 0, 0, jnp.where(i < share, share * shards - 1, in_rest))

    last_step = (n - 1) * chunks - 1
    inner_done = (n - 2) * chunks - 1
    third_at = jnp.where(is_end, last_step - 4, inner_done + 1)
    early_at = last_step - jnp.where(is_end, 4, 3)
    low_at = jnp.maximum(jnp.maximum(low_ready(0), low_ready(1)), chunks)

    own_pair = t // 2

    def pair_rows(m):
        start = m * 2 * rows
        return pl.ds(start if isinstance(m, int) else pl.multiple_of(start, 2 * rows), 2 * rows)

    def part_copy(m):
        return pltpu.make_async_remote_copy(
            src_ref=low_part.at[pair_rows(m), :],
            dst_ref=low_got.at[t],
            send_sem=part_send.at[m],
            recv_sem=part_recv.at[t],
            device_id={"tensor": owners[m]},
            device_id_type=MESH,
        )

    def part_arrival(d):
        source = lax.rem(t + n - d, n)
        return pltpu.make_async_remote_copy(
            src_ref=low_got.at[source],
            dst_ref=low_got.at[source],
            send_sem=part_send.at[0],
            recv_sem=part_recv.at[source],
            device_id={"tensor": source},
            device_id_type=MESH,
        )

    def low_copy(d):
        held = low_all.at[pair_rows(own_pair), :]
        return pltpu.make_async_remote_copy(
            src_ref=held,
            dst_ref=held,
            send_sem=low_send.at[d],
            recv_sem=low_recv.at[own_pair],
            device_id={"tensor": lax.rem(t + d, n)},
            device_id_type=MESH,
        )

    def low_arrival(m):
        held = low_all.at[pair_rows(m), :]
        return pltpu.make_async_remote_copy(
            src_ref=held,
            dst_ref=held,
            send_sem=low_send.at[0],
            recv_sem=low_recv.at[m],
            device_id={"tensor": owners[m]},
            device_id_type=MESH,
        )

    def adapters_arrive():
        for d in range(1, stores):
            source = lax.rem(s + stores - d, stores)
            for i, (_, held) in enumerate(adapter_pairs):
                block = adapter_block(held, i, source)
                pltpu.make_async_remote_copy(
                    src_ref=block,
                    dst_ref=block,
                    send_sem=adapter_send.at[i, d],
                    recv_sem=adapter_recv.at[i, d],
                    device_id={"store": source},
                    device_id_type=MESH,
                ).wait_recv()

    def low_first():
        fill_holder()
        adapters_arrive()
        summed = jnp.zeros(low_part.shape, jnp.float32)
        for p in range(stores):
            picked = jnp.zeros(low_part.shape, jnp.float32)
            for k in range(share):
                picked += lax.dot_general(
                    xbuf[t * share + k],
                    down[p, :, k * width : (k + 1) * width],
                    (((1,), (1,)), ((), ())),
                    preferred_element_type=jnp.float32,
                )
            summed += picked * mask_of(p)
        low_part[...] = summed.astype(jnp.bfloat16)
        low_own[...] = summed
        for m in range(pairs):

            @pl.when(t != owners[m])
            def _():
                part_copy(m).start()

    def low_second():
        at = pair_rows(own_pair)
        whole = low_own[at, :]
        for d in range(1, n):
            part_arrival(d).wait_recv()
            whole += low_got[lax.rem(t + n - d, n)].astype(jnp.float32)
        low_all[at, :] = whole.astype(jnp.bfloat16)
        for d in range(1, n):
            low_copy(d).start()

    def spread_low(lower):
        low = low_all[...].astype(jnp.float32)
        turned = pltpu.roll(low, ADAPTER_RANK, 1)
        in_lower = lax.broadcasted_iota(jnp.int32, low.shape, 1) < ADAPTER_RANK
        twice = jnp.where(in_lower, low, turned) if lower else jnp.where(in_lower, turned, low)
        masks = [
            jnp.where(in_lower, mask_of(2 * p), mask_of(2 * p + 1)) for p in range(stores // 2)
        ]
        return jnp.concatenate([(twice * m).astype(jnp.bfloat16) for m in masks], axis=1)

    def low_keyval():
        for m in range(pairs):

            @pl.when(t != owners[m])
            def _():
                low_arrival(m).wait_recv()

        acc_kv[...] += adapter_scale * jnp.dot(
            spread_low(False), upkv[...], preferred_element_type=jnp.float32
        )

    def low_query():
        spread = spread_low(True)
        for k in range(query_width // tile_q):
            columns = slice(k * tile_q, (k + 1) * tile_q)
            acc_q[:, columns] += adapter_scale * jnp.dot(
                spread, upq[:, columns], preferred_element_type=jnp.float32
            )

    def rotated(value, cosine, sine):
        return value * cosine + pltpu.roll(value, HEAD_SIZE // 2, 1) * sine

    ends_first = t >= n - t
    early_start = pl.multiple_of(jnp.where(ends_first, rows, 0), rows)
    late_start = pl.multiple_of(jnp.where(ends_first, 0, total - rows), rows)
    partner = t + 1 - 2 * (t % 2)

    def finish_keyval(start, count):
        at = pl.ds(start, count)
        cosine = jnp.where(holds_keys, cos_ref[at, :], 1.0)
        sine = jnp.where(holds_keys, sin_ref[at, :], 0.0)
        for m in range(pair_heads):
            value = acc_kv[at, m * HEAD_SIZE : (m + 1) * HEAD_SIZE]
            kv_heads[m, at, :] = rotated(value, cosine, sine).astype(jnp.bfloat16)

    def keyval_copy(start, count, which):
        at = pl.ds(start, count)
        return pltpu.make_async_remote_copy(
            src_ref=kv_heads.at[pl.ds(kv_first(partner), kv_used), at, :],
            dst_ref=kv_got.at[:, at, :],
            send_sem=kv_sem.at[0, which],
            recv_sem=kv_sem.at[1, which],
            device_id={"tensor": partner},
            device_id_type=MESH,
        )

    own_first = kv_first(t)
    is_inner = jnp.logical_not(is_end)
    starts_first = jnp.logical_not(ends_first)
    holds_values = jnp.logical_not(holds_keys)
    early_count = total - rows
    per_kv = head_local // kv_used
    batch = min(8, per_kv)
    block = 128
    blocks = total // block
    scale = 1.0 / math.sqrt(HEAD_SIZE) / math.log(2.0)
    stage_at = pl.multiple_of(jnp.where(ends_first, model_width - total, 0), total)
    part_at = pl.multiple_of(jnp.where(ends_first, model_width - 2 * total, total), total)

    def finish_late():
        finish_keyval(late_start, rows)
        keyval_copy(late_start, rows, 1).start()

    def gather_keys(start, count):
        at = pl.ds(start, count)
        for g in range(kv_used):

            @pl.when(holds_keys)
            def _():
                keys_ref[g, at, :] = kv_heads[own_first + g, at, :]

            @pl.when(holds_values)
            def _():
                keys_ref[g, at, :] = kv_got[g, at, :]

    def gather_values(start, count):
        at = pl.ds(start, count)
        for g in range(kv_used):

            @pl.when(holds_keys)
            def _():
                values_ref[g, at, :HEAD_SIZE] = kv_got[g, at, :]

            @pl.when(holds_values)
            def _():
                values_ref[g, at, :HEAD_SIZE] = kv_heads[own_first + g, at, :]

    def lanes_of(h):
        return pl.ds(pl.multiple_of(h * HEAD_SIZE, HEAD_SIZE), HEAD_SIZE)

    def stage_rows(start, first, count):
        return pl.ds(pl.multiple_of(start + first, block), count)

    def scores_of(b, g, lanes, low, high):
        at = slice(b * block, (b + 1) * block)
        query = [
            rotated(acc_q[at, ln], cos_ref[at, :], sin_ref[at, :]).astype(jnp.bfloat16)
            for ln in lanes
        ]
        scores = lax.dot_general(
            jnp.concatenate(query, axis=0),
            keys_ref[g, low:high, :],
            (((1,), (1,)), ((), ())),
            preferred_element_type=jnp.float32,
        )
        scores = scores.reshape(2, block, high - low) + bias_ref[at, low:high][None]
        return scores.reshape(2 * block, high - low)

    def weights_of(b, g, lanes):
        scores = scores_of(b, g, lanes, max(0, b * block - MAX_RUN), (b + 1) * block)
        scores = (scores - jnp.max(scores, axis=1, keepdims=True)) * scale
        return jnp.exp2(scores).astype(jnp.bfloat16)

    def attend(b, g, lanes):
        low = max(0, b * block - MAX_RUN)
        high = (b + 1) * block
        mixed = jnp.dot(
            weights_of(b, g, lanes), values_ref[g, low:high, :], preferred_element_type=jnp.float32
        )
        mixed = (mixed[:, :HEAD_SIZE] / mixed[:, HEAD_SIZE:]).astype(jnp.bfloat16)
        for k, ln in enumerate(lanes):
            wq[stage_rows(stage_at, b * block, block), ln] = mixed[k * block : (k + 1) * block]

    def attend_part(b, g, lanes):
        high = (b + 1) * block
        weights = weights_of(b, g, lanes)
        first = weights[:, :block]
        sums = jnp.dot(
            first, values_ref[g, :block, HEAD_SIZE:], preferred_element_type=jnp.float32
        )
        if b > 0:
            mixed = jnp.dot(
                weights[:, block:], values_ref[g, block:high, :], preferred_element_type=jnp.float32
            )
            sums += mixed[:, HEAD_SIZE:]
        inverse = 1.0 / sums
        rest = mixed[:, :HEAD_SIZE] * inverse if b > 0 else jnp.zeros_like(inverse)
        first = (first.astype(jnp.float32) * inverse).astype(jnp.bfloat16)
        for k, ln in enumerate(lanes):
            acc_q[b * block : high, ln] = rest[k * block : (k + 1) * block]
            wq[stage_rows(part_at, b * block, block), ln] = first[k * block : (k + 1) * block]

    def attend_rest(b, g, lanes):
        ln = pl.ds(lanes[0].start, 2 * HEAD_SIZE)
        first, count = b * block, (blocks - 1 - b) * block
        more = jnp.dot(
            wq[stage_rows(part_at, first, count), ln],
            twin_ref[g],
            preferred_element_type=jnp.float32,
        )
        whole = acc_q[first : first + count, ln] + more
        wq[stage_rows(stage_at, first, count), ln] = whole.astype(jnp.bfloat16)

    last = (blocks - 1) * block
    kept = [slice(k * block, (k + 1) * block) for k in range(3)]

    def attend_start(g, lanes):
        scores = scores_of(blocks - 1, g, lanes, last - MAX_RUN, last)
        top = jnp.max(scores, axis=1, keepdims=True)
        weights = jnp.exp2((scores - top) * scale).astype(jnp.bfloat16)
        mixed = jnp.dot(
            weights, values_ref[g, last - MAX_RUN : last, :], preferred_element_type=jnp.float32
        )
        for k, ln in enumerate(lanes):
            at = slice(k * block, (k + 1) * block)
            acc_q[kept[0], ln] = mixed[at, :HEAD_SIZE]
            acc_q[kept[1], ln] = mixed[at, HEAD_SIZE:]
            acc_q[kept[2], ln] = jnp.broadcast_to(top[at], (block, HEAD_SIZE))

    def attend_finish(g, lanes):
        scores = scores_of(blocks - 1, g, lanes, last, total)
        total_of, sum_of, top_of = (
            jnp.concatenate([acc_q[at, ln] for ln in lanes], axis=0) for at in kept
        )
        top = jnp.maximum(top_of, jnp.max(scores, axis=1, keepdims=True))
        weights = jnp.exp2((scores - top) * scale).astype(jnp.bfloat16)
        shrink = jnp.exp2((top_of - top) * scale)
        mixed = jnp.dot(
            weights, values_ref[g, last:total, :], preferred_element_type=jnp.float32
        )
        sums = sum_of * shrink + mixed[:, HEAD_SIZE:]
        mixed = ((total_of * shrink + mixed[:, :HEAD_SIZE]) / sums).astype(jnp.bfloat16)
        for k, ln in enumerate(lanes):
            wq[stage_rows(stage_at, last, block), ln] = mixed[k * block : (k + 1) * block]

    cut = total - block

    def out_copy(q, which):
        first, count = (0, cut) if which == 0 else (cut, block)
        lanes = pl.ds(pl.multiple_of(q * batch * HEAD_SIZE, batch * HEAD_SIZE), batch * HEAD_SIZE)
        return pltpu.make_async_copy(
            wq.at[stage_rows(stage_at, first, count), lanes],
            out_ref.at[pl.ds(first, count), lanes],
            out_sem.at[which, q],
        )

    def heads(body, which, q):
        g = q * batch // per_kv
        for pair in range(batch // 2):
            body(g, [lanes_of(q * batch + 2 * pair + k) for k in range(2)])
        out_copy(q, which).start()

    def over_heads(body, which):
        @pl.loop(0, head_local // batch)
        def _(q):
            heads(body, which, q)

    def early_keyval():
        keyval_copy(early_start, early_count, 0).wait_recv()
        gather_keys(early_start, early_count)
        gather_values(early_start, early_count)

        @pl.when(ends_first)
        def _():
            @pl.when(holds_values)
            def _():
                keyval_copy(late_start, rows, 1).wait_recv()

            gather_keys(late_start, rows)

    def early_attention(q):
        def lower(inner):
            def body(g, lanes):
                for b in range(blocks - 1):
                    attend(b, g, lanes)
                if inner:
                    attend_start(g, lanes)

            return body

        def upper(inner):
            def body(g, lanes):
                attend(blocks - 1, g, lanes)
                for b in range(0 if inner else 1, blocks - 1):
                    attend_part(b, g, lanes)

            return body

        for inner, where in ((False, is_end), (True, is_inner)):

            @pl.when(jnp.logical_and(where, starts_first))
            def _():
                heads(lower(inner), 0, q)

            @pl.when(jnp.logical_and(where, ends_first))
            def _():
                heads(upper(inner), 1, q)

    def late_attention():
        def lower(inner):
            def body(g, lanes):
                if inner:
                    attend_finish(g, lanes)
                else:
                    attend(blocks - 1, g, lanes)

            return body

        def upper(inner):
            def body(g, lanes):
                if not inner:
                    attend(0, g, lanes)
                attend_rest(0 if inner else 1, g, lanes)

            return body

        @pl.when(starts_first)
        def _():
            keyval_copy(late_start, rows, 1).wait_recv()
            gather_keys(late_start, rows)
            gather_values(late_start, rows)

        @pl.when(ends_first)
        def _():
            @pl.when(holds_keys)
            def _():
                keyval_copy(late_start, rows, 1).wait_recv()

            gather_values(late_start, rows)
            for g in range(kv_used):
                value = values_ref[g, :block, :HEAD_SIZE]
                twin_ref[g, :block, :HEAD_SIZE] = value
                twin_ref[g, block:, HEAD_SIZE:] = value

        for inner, where in ((False, is_end), (True, is_inner)):

            @pl.when(jnp.logical_and(where, starts_first))
            def _():
                over_heads(lower(inner), 1)

            @pl.when(jnp.logical_and(where, ends_first))
            def _():
                over_heads(upper(inner), 0)

    twin_ref[...] = jnp.zeros_like(twin_ref)
    for g in range(kv_used):
        values_ref[g, :, HEAD_SIZE:] = jnp.ones((total, HEAD_SIZE), jnp.bfloat16)

    @pl.loop(0, last_step)
    def _(step):
        here = tuple(step < reach[side] * chunks for side in range(2))
        places = [item(reach[side], step) for side in range(2)]
        for side in range(2):
            p, i = places[side]

            @pl.when(here[side])
            def _():
                arrival(side, p, i).wait_recv()

            sends = (reach[side] + 1) * chunks
            head = (reach[side] + 1) * share

            @pl.when(jnp.logical_and(can_send[side], step + depth - 1 < sends))
            def _():
                send_item(side, step, False).wait_send()

                @pl.when(step + ahead <= head)
                def _():
                    start_send(side, step + ahead)

                @pl.when(step + ahead == head)
                def _():
                    for j in range(1, depth - 1):
                        start_send(side, step + ahead + j)

                nearer = step > inner_done
                later = step + depth - jnp.where(nearer, 1, 0)
                wanted = jnp.logical_and(step + ahead > head, step != inner_done + 1)

                @pl.when(jnp.logical_and(wanted, later < sends))
                def _():
                    start_send(side, later)

        @pl.when(step < chunks // 2)
        def _():
            for c in (step, chunks - 1 - step):
                for copy in weight_copies(c):
                    copy.wait()

            @pl.when(step + 1 < chunks // 2)
            def _():
                start_weights(step + 1)

        for side in range(2):
            p, i = places[side]

            @pl.when(here[side])
            def _():
                keyval_unit(place(side, i), t - p if side == 0 else t + p)

        for side in range(2):
            p, i = places[side]

            @pl.when(here[side])
            def _():
                query_unit(place(side, i), t - p if side == 0 else t + p)

        @pl.when(jnp.logical_and(step >= chunks, step < 2 * chunks))
        def _():
            keyval_unit(step - chunks, t)
            query_unit(step - chunks, t)

        @pl.when(step == chunks - 2)
        def _():
            fill_tables()

        @pl.when(step == low_at)
        def _():
            low_first()

        @pl.when(jnp.logical_and(is_owner, step == inner_done))
        def _():
            low_second()

        @pl.when(step == third_at)
        def _():
            low_keyval()
            finish_keyval(early_start, early_count)
            keyval_copy(early_start, early_count, 0).start()

            @pl.when(is_inner)
            def _():
                finish_late()

            low_query()

        @pl.when(step == early_at)
        def _():
            early_keyval()

        @pl.when(jnp.logical_and(step >= early_at, step < early_at + head_local // batch))
        def _():
            early_attention(step - early_at)

    @pl.when(is_end)
    def _():
        at = pl.ds(late_start, rows)
        for h in range(2):
            half_copy(h).wait_recv()
            part = pl.ds(pl.multiple_of(last_chunk * width + h * half, half), half)
            x = xbuf[last_chunk, at, h * half : (h + 1) * half]
            acc_kv[at, :] += jnp.dot(x, wkv[part, :], preferred_element_type=jnp.float32)
            if h == 1:
                finish_late()

            @pl.loop(0, query_width // tile_q)
            def _(k):
                columns = pl.ds(pl.multiple_of(k * tile_q, tile_q), tile_q)
                acc_q[at, columns] += jnp.dot(
                    xbuf[last_chunk, at, h * half : (h + 1) * half],
                    wq[part, columns],
                    preferred_element_type=jnp.float32,
                )

    late_attention()

    for copy in adapter_sends:
        copy.wait_send()
    for m in range(pairs):

        @pl.when(t != owners[m])
        def _():
            part_copy(m).wait_send()

    @pl.when(is_owner)
    def _():
        for d in range(1, n):
            low_copy(d).wait_send()

    keyval_copy(early_start, early_count, 0).wait_send()
    keyval_copy(late_start, rows, 1).wait_send()

    for side in range(2):

        @pl.when(can_send[side])
        def _():
            for j in range(1, depth - 1):
                send_item(side, (reach[side] + 1) * chunks - depth + j, False).wait_send()

            @pl.when(reach[side] < n - 2)
            def _():
                send_item(side, (reach[side] + 1) * chunks - 1, False).wait_send()

            @pl.when(reach[side] == n - 2)
            def _():
                for h in range(2):
                    half_copy(h).wait_send()

    @pl.loop(0, head_local // batch)
    def _(q):
        for which in range(2):
            out_copy(q, which).wait()


def on_device(
    tokens,
    query_weight,
    key_value_weight,
    adapter_down_maps,
    adapter_up_query,
    adapter_up_key_value,
    adapter_row_table,
    request_adapter_ids,
    token_request_ids,
):
    n = lax.axis_size("tensor")
    stores = lax.axis_size("store")
    slots = adapter_down_maps.shape[0]
    rows, model_width = tokens.shape
    total = rows * n
    query_width = query_weight.shape[1]
    keyval_width = key_value_weight.shape[1]
    chunks = max(8, 2 * n)
    width = model_width // chunks
    pair_heads = keyval_width // HEAD_SIZE
    kv_used = max(query_width // HEAD_SIZE // (QUERY_HEADS // KEY_VALUE_HEADS), 1)
    two_ranks = 2 * ADAPTER_RANK
    hbm = pl.BlockSpec(memory_space=pl.ANY)
    vmem = pl.BlockSpec(memory_space=pltpu.VMEM)
    smem = pl.BlockSpec(memory_space=pltpu.SMEM)
    dma = pltpu.SemaphoreType.DMA
    results = pl.pallas_call(
        functools.partial(project_kernel, n, stores, chunks, slots),
        in_specs=[hbm] * 6 + [smem, smem, vmem],
        out_specs=[hbm] * 4,
        out_shape=[
            jax.ShapeDtypeStruct((total, query_width), jnp.bfloat16),
            jax.ShapeDtypeStruct((stores, two_ranks, query_width), jnp.bfloat16),
            jax.ShapeDtypeStruct((stores, ADAPTER_RANK, query_width), jnp.bfloat16),
            jax.ShapeDtypeStruct((stores, ADAPTER_RANK, keyval_width), jnp.bfloat16),
        ],
        scratch_shapes=[
            pltpu.VMEM((chunks, total, width), jnp.bfloat16),
            pltpu.VMEM((model_width, query_width), jnp.bfloat16),
            pltpu.VMEM((model_width, keyval_width), jnp.bfloat16),
            pltpu.VMEM((total, query_width), jnp.float32),
            pltpu.VMEM((total, keyval_width), jnp.float32),
            pltpu.VMEM((stores, two_ranks, model_width // n), jnp.bfloat16),
            pltpu.VMEM((stores * ADAPTER_RANK, query_width), jnp.bfloat16),
            pltpu.VMEM((stores * ADAPTER_RANK, keyval_width), jnp.bfloat16),
            pltpu.VMEM((total, two_ranks), jnp.bfloat16),
            pltpu.VMEM((total, two_ranks), jnp.float32),
            pltpu.VMEM((n, 2 * rows, two_ranks), jnp.bfloat16),
            pltpu.VMEM((total, two_ranks), jnp.bfloat16),
            pltpu.VMEM((pair_heads, total, HEAD_SIZE), jnp.bfloat16),
            pltpu.VMEM((kv_used, total, HEAD_SIZE), jnp.bfloat16),
            pltpu.VMEM((kv_used, total, HEAD_SIZE), jnp.bfloat16),
            pltpu.VMEM((kv_used, total, 2 * HEAD_SIZE), jnp.bfloat16),
            pltpu.VMEM((kv_used, 2 * HEAD_SIZE, 2 * HEAD_SIZE), jnp.bfloat16),
            pltpu.VMEM((total, total), jnp.float32),
            pltpu.VMEM((total, HEAD_SIZE), jnp.float32),
            pltpu.VMEM((total, HEAD_SIZE), jnp.float32),
            pltpu.VMEM((total, 1), jnp.float32),
            dma((chunks,)),
            dma((2, chunks)),
            dma((2, n, chunks)),
            dma((2, n, chunks)),
            dma((3, stores)),
            dma((3, stores)),
            dma((3,)),
            dma((3, slots)),
            dma((3, stores)),
            dma((n,)),
            dma((n,)),
            dma((n,)),
            dma((n,)),
            dma((2, 2)),
            dma((2, 2)),
            dma((2, query_width // HEAD_SIZE)),
        ],
        compiler_params=pltpu.CompilerParams(
            collective_id=0, has_side_effects=True, vmem_limit_bytes=67043328
        ),
        name="project",
    )(
        tokens,
        query_weight,
        key_value_weight,
        adapter_down_maps,
        adapter_up_query,
        adapter_up_key_value,
        adapter_row_table,
        request_adapter_ids,
        token_request_ids,
    )
    return hand_over(results[0])


def hand_over_kernel(pieces, source, out, held, in_sem, out_sem):
    count = held.shape[0] // pieces

    def load(k):
        at = pl.ds(k * count, count)
        return pltpu.make_async_copy(source.at[at, :], held.at[at, :], in_sem.at[k])

    def store(k):
        at = pl.ds(k * count, count)
        return pltpu.make_async_copy(held.at[at, :], out.at[at, :], out_sem.at[k])

    for k in range(pieces):
        load(k).start()
    for k in range(pieces):
        load(k).wait()
        store(k).start()
    for k in range(pieces):
        store(k).wait()


def hand_over(attention):
    hbm = pl.BlockSpec(memory_space=pl.ANY)
    pieces = 8
    return pl.pallas_call(
        functools.partial(hand_over_kernel, pieces),
        in_specs=[hbm],
        out_specs=hbm,
        out_shape=jax.ShapeDtypeStruct(attention.shape, attention.dtype),
        scratch_shapes=[
            pltpu.VMEM(attention.shape, attention.dtype),
            pltpu.SemaphoreType.DMA((pieces,)),
            pltpu.SemaphoreType.DMA((pieces,)),
        ],
        name="hand_over",
    )(attention)


def solution(mesh):
    return jax.shard_map(
        on_device,
        mesh=mesh,
        in_specs=(
            P(("groups", "store", "tensor"), None),
            P(None, "tensor"),
            P(None, "tensor"),
            P("store", None, "tensor"),
            P("store", None, "tensor"),
            P("store", None, "tensor"),
            P("groups"),
            P("groups", None),
            P(("groups", "store"), None),
        ),
        out_specs=P(("groups", "store"), "tensor"),
        check_vma=False,
    )
```

```python
import functools
import math

import jax
import jax.numpy as jnp
from jax import lax
from jax.experimental import pallas as pl
from jax.experimental.pallas import tpu as pltpu
from jax.sharding import PartitionSpec as P

MODEL_WIDTH = 8192
QUERY_HEADS = 64
KEY_VALUE_HEADS = 8
HEAD_SIZE = 128
ADAPTER_RANK = 64
STORE_REQUESTS = 4
TOK_ST = 512


adapter_scale = 2.0
rope_theta = 500000.0


MAX_RUN = 256
MESH = pl.DeviceIdType.MESH


def project_kernel(
    n,
    stores,
    chunks,
    slots,
    tokens_ref,
    wq_hbm,
    wkv_hbm,
    down_hbm,
    upq_hbm,
    upkv_hbm,
    table_ref,
    request_ref,
    segment_ref,
    out_ref,
    down_picked,
    upq_picked,
    upkv_picked,
    xbuf,
    wq,
    wkv,
    acc_q,
    acc_kv,
    down,
    upq,
    upkv,
    low_part,
    low_own,
    low_got,
    low_all,
    kv_heads,
    kv_got,
    keys_ref,
    values_ref,
    twin_ref,
    twin_keys_ref,
    bias_ref,
    cos_ref,
    sin_ref,
    holder_ref,
    token_sem,
    weight_sem,
    recv_sem,
    send_sem,
    adapter_send,
    adapter_recv,
    adapter_own,
    candidate_sem,
    picked_sem,
    part_send,
    part_recv,
    low_send,
    low_recv,
    kv_sem,
    half_sem,
    out_sem,
):
    t = lax.axis_index("tensor")
    s = lax.axis_index("store")
    rows = tokens_ref.shape[0]
    width = tokens_ref.shape[1] // chunks
    total = rows * n
    query_width = wq.shape[1]
    keyval_width = wkv.shape[1]
    pair_heads = keyval_width // HEAD_SIZE
    head_local = query_width // HEAD_SIZE
    group_size = QUERY_HEADS // KEY_VALUE_HEADS
    kv_used = max(head_local // group_size, 1)

    def kv_first(rank):
        return rank * head_local // group_size - rank // 2 * pair_heads

    barrier = pltpu.get_barrier_semaphore()
    pairs = n // 2
    owners = [2 * m + 1 if 2 * m + 1 < n - 2 * m - 1 else 2 * m for m in range(pairs)]

    def owns(rank):
        m = rank // 2
        return rank == 2 * m + jnp.where(2 * m + 1 < n - 2 * m - 1, 1, 0)

    is_owner = owns(t)
    greeted = 0
    for d in range(1, n):
        peer = lax.rem(t + d, n)
        near = jnp.logical_or(peer == t + 1, peer == t - 1)
        meets = jnp.logical_or(near, jnp.logical_or(is_owner, owns(peer)))
        greeted += jnp.where(meets, 1, 0)

        @pl.when(meets)
        def _():
            pl.semaphore_signal(
                barrier, inc=1, device_id={"tensor": peer}, device_id_type=MESH
            )

    for d in range(1, stores):
        pl.semaphore_signal(
            barrier, inc=1, device_id={"store": lax.rem(s + d, stores)}, device_id_type=MESH
        )

    def own_copy(c):
        return pltpu.make_async_copy(
            tokens_ref.at[:, pl.ds(c * width, width)],
            xbuf.at[c, pl.ds(t * rows, rows), :],
            token_sem.at[c],
        )

    def weight_copies(c):
        part = pl.ds(c * width, width)
        return (
            pltpu.make_async_copy(wq_hbm.at[part, :], wq.at[part, :], weight_sem.at[0, c]),
            pltpu.make_async_copy(wkv_hbm.at[part, :], wkv.at[part, :], weight_sem.at[1, c]),
        )

    model_width = wq.shape[0]
    two_ranks = 2 * ADAPTER_RANK
    picked_down = chunks // 2 * width
    picked_up = picked_down + stores * two_ranks
    picked_end = picked_up + stores * ADAPTER_RANK
    candidate_sets = (
        (down_hbm, wq, 0, two_ranks, picked_down, down_picked),
        (upq_hbm, wq, slots * two_ranks, ADAPTER_RANK, picked_up, upq_picked),
        (upkv_hbm, wkv, 0, ADAPTER_RANK, picked_up, upkv_picked),
    )
    candidates = [
        pltpu.make_async_copy(
            source.at[k], held.at[pl.ds(first + k * count, count), :], candidate_sem.at[j, k]
        )
        for j, (source, held, first, count, _, _) in enumerate(candidate_sets)
        for k in range(slots)
    ]
    adapter_pairs = ((down_picked, down), (upq_picked, upq), (upkv_picked, upkv))

    def adapter_block(held, i, at):
        if i == 0:
            return held.at[at]
        return held.at[pl.ds(at * ADAPTER_RANK, ADAPTER_RANK), :]

    own_adapters = [
        pltpu.make_async_copy(source.at[s], adapter_block(held, i, s), adapter_own.at[i])
        for i, (source, held) in enumerate(adapter_pairs)
    ]

    pl.semaphore_wait(barrier, greeted + stores - 1)

    def place(side, i):
        return chunks - 1 - i if side == 0 else i

    def stream_copy(side, p, i, own):
        c = place(side, i)
        shard = t - p if side == 0 else t + p
        held = xbuf.at[c, pl.ds(shard * rows, rows), :]
        source = tokens_ref.at[:, pl.ds(c * width, width)] if own else held
        return pltpu.make_async_remote_copy(
            src_ref=source,
            dst_ref=held,
            send_sem=send_sem.at[side, p, i],
            recv_sem=recv_sem.at[side, p, i],
            device_id={"tensor": t + 1 if side == 0 else t - 1},
            device_id_type=MESH,
        )

    def arrival(side, p, i):
        c = place(side, i)
        shard = t - p if side == 0 else t + p
        held = xbuf.at[c, pl.ds(shard * rows, rows), :]
        return pltpu.make_async_remote_copy(
            src_ref=held,
            dst_ref=held,
            send_sem=send_sem.at[side, p - 1, i],
            recv_sem=recv_sem.at[side, p - 1, i],
            device_id={"tensor": t - 1 if side == 0 else t + 1},
            device_id_type=MESH,
        )

    is_end = jnp.logical_or(t == 0, t == n - 1)
    share = chunks // n
    can_send = (t < n - 1, t > 0)
    reach = (t, n - 1 - t)

    def item(shards, j):
        head = share * shards
        rest = chunks - share
        in_head = j < head
        k = jnp.maximum(j - head, 0)
        return (
            jnp.where(in_head, j // share, k // rest) + 1,
            jnp.where(in_head, j % share, share + k % rest),
        )

    def send_item(side, j, own):
        p, i = item(reach[side] + 1, j)
        return stream_copy(side, p - 1, i, own)

    half = width // 2
    last_chunk = jnp.where(t >= n - t, 0, chunks - 1)
    last_shard = jnp.where(t >= n - t, 0, n - 1)
    outward = jnp.where(t >= n - t, t + 1, t - 1)

    def half_copy(h):
        held = xbuf.at[
            last_chunk,
            pl.ds(pl.multiple_of(last_shard * rows, rows), rows),
            pl.ds(h * half, half),
        ]
        return pltpu.make_async_remote_copy(
            src_ref=held,
            dst_ref=held,
            send_sem=half_sem.at[0, h],
            recv_sem=half_sem.at[1, h],
            device_id={"tensor": jnp.where(is_end, t + 1 - 2 * (t % 2), outward)},
            device_id_type=MESH,
        )

    def start_send(side, j):
        p, i = item(reach[side] + 1, j)
        is_last = jnp.logical_and(p == n - 1, i == chunks - 1)

        @pl.when(is_last)
        def _():
            for h in range(2):
                half_copy(h).start()

        @pl.when(p == 1)
        def _():
            stream_copy(side, 0, i, True).start()

        @pl.when(jnp.logical_and(p > 1, jnp.logical_not(is_last)))
        def _():
            stream_copy(side, p - 1, i, False).start()

    ahead = 2
    depth = 4
    for j in range(ahead):
        for side in range(2):

            @pl.when(can_send[side])
            def _():
                stream_copy(side, 0, j, True).start()

    for copy in candidates:
        copy.start()
    for c in range(chunks):
        own_copy(c).start()

    tile_q = min(query_width, 512)

    def keyval_unit(c, shard):
        at = pl.ds(pl.multiple_of(shard * rows, rows), rows)
        part = pl.ds(pl.multiple_of(c * width, width), width)
        acc_kv[at, :] += jnp.dot(
            xbuf[c, at, :], wkv[part, :], preferred_element_type=jnp.float32
        )

    def query_unit(c, shard):
        at = pl.ds(pl.multiple_of(shard * rows, rows), rows)
        part = pl.ds(pl.multiple_of(c * width, width), width)

        @pl.loop(0, query_width // tile_q)
        def _(k):
            columns = pl.ds(pl.multiple_of(k * tile_q, tile_q), tile_q)
            acc_q[at, columns] += jnp.dot(
                xbuf[c, at, :], wq[part, columns], preferred_element_type=jnp.float32
            )

    acc_q[...] = jnp.zeros_like(acc_q)
    acc_kv[...] = jnp.zeros_like(acc_kv)
    holds_keys = t % 2 == 0

    def request_column():
        place_row = lax.broadcasted_iota(jnp.int32, (total, total), 0)
        place_column = lax.broadcasted_iota(jnp.int32, (total, total), 1)
        across = segment_ref[...].astype(jnp.float32)
        own = jnp.where(place_row == place_column, across, 0.0)
        return across, jnp.sum(own, axis=1, keepdims=True), place_row >= place_column

    def fill_tables():
        across, down_column, ordered = request_column()
        allowed = jnp.logical_and(down_column == across, ordered)
        bias_ref[...] = jnp.where(allowed, 0.0, -1e30)
        first_index = jnp.sum(jnp.where(across < down_column, 1.0, 0.0), axis=1, keepdims=True)
        place_token = lax.broadcasted_iota(jnp.int32, (total, 1), 0).astype(jnp.float32)
        lane = lax.broadcasted_iota(jnp.int32, (total, HEAD_SIZE), 1)
        exponent = lax.rem(lane, HEAD_SIZE // 2).astype(jnp.float32) * (2.0 / HEAD_SIZE)
        angles = (place_token - first_index) * jnp.exp(-exponent * math.log(rope_theta))
        sine = jnp.sin(angles)
        cos_ref[...] = jnp.cos(angles)
        sin_ref[...] = jnp.where(lane < HEAD_SIZE // 2, -sine, sine)

    def fill_holder():
        _, down_column, _ = request_column()
        holder = jnp.zeros((total, 1), jnp.float32)
        for k in range(STORE_REQUESTS):
            owner = lax.div(table_ref[request_ref[s, k]], slots).astype(jnp.float32)
            holder += jnp.where(down_column == float(k), owner, 0.0)
        holder_ref[...] = holder

    for copy in candidates:
        copy.wait()
    bits = []
    for i in range(stores):
        index = 0
        for k in range(STORE_REQUESTS):
            slot = table_ref[request_ref[i, k]]
            index += jnp.where(lax.div(slot, slots) == s, lax.rem(slot, slots), 0)
        bits.append([lax.rem(lax.div(index, 1 << k), 2) == 1 for k in range(slots.bit_length())])

    def pick(held, first, count, to):
        lanes = min(held.shape[1], 512)

        @pl.loop(0, count // 16)
        def _(r):
            for at in range(0, held.shape[1], lanes):
                columns = slice(at, at + lanes)

                def tile(base, k):
                    return pl.ds(pl.multiple_of(base + k * count + r * 16, 16), 16)

                found = [held[tile(first, k), columns] for k in range(slots)]
                for i in range(stores):
                    left, level = found, 0
                    while len(left) > 1:
                        bit = bits[i][level]
                        left = [
                            jnp.where(bit, left[k + 1], left[k]) if k + 1 < len(left) else left[k]
                            for k in range(0, len(left), 2)
                        ]
                        level += 1
                    held[tile(to, i), columns] = left[0]

    for _, held, first, count, to, _ in candidate_sets:
        pick(held, first, count, to)
    picked_copies = [
        pltpu.make_async_copy(
            held.at[pl.ds(to + i * count, count), :], picked.at[i], picked_sem.at[j, i]
        )
        for j, (_, held, _, count, to, picked) in enumerate(candidate_sets)
        for i in range(stores)
    ]
    for copy in picked_copies:
        copy.start()
    def start_weights(k):
        for c in (k, chunks - 1 - k):
            for copy in weight_copies(c):
                copy.start()

    start_weights(0)
    for copy in picked_copies:
        copy.wait()
    for copy in own_adapters:
        copy.start()
    adapter_sends = []
    for d in range(1, stores):
        for i, (source, held) in enumerate(adapter_pairs):
            peer = lax.rem(s + d, stores)
            copy = pltpu.make_async_remote_copy(
                src_ref=source.at[peer],
                dst_ref=adapter_block(held, i, s),
                send_sem=adapter_send.at[i, d],
                recv_sem=adapter_recv.at[i, d],
                device_id={"store": peer},
                device_id_type=MESH,
            )
            copy.start()
            adapter_sends.append(copy)


    def mask_of(p):
        return jnp.where(holder_ref[...] == float(p), 1.0, 0.0)

    for copy in own_adapters:
        copy.wait()
    for c in range(chunks):
        own_copy(c).wait()

    def low_ready(side):
        first = share * (t if side == 1 else n - 1 - t)
        i = first + share - 1
        shards = reach[side]
        in_rest = share * shards + (shards - 1) * (chunks - share) + i - share
        return jnp.where(shards == 0, 0, jnp.where(i < share, share * shards - 1, in_rest))

    last_step = (n - 1) * chunks - 1
    inner_done = (n - 2) * chunks - 1
    third_at = jnp.where(is_end, last_step - 4, inner_done + 1)
    early_at = last_step - jnp.where(is_end, 4, 3)
    low_at = jnp.maximum(jnp.maximum(low_ready(0), low_ready(1)), chunks)

    own_pair = t // 2

    def pair_rows(m):
        start = m * 2 * rows
        return pl.ds(start if isinstance(m, int) else pl.multiple_of(start, 2 * rows), 2 * rows)

    def part_copy(m):
        return pltpu.make_async_remote_copy(
            src_ref=low_part.at[pair_rows(m), :],
            dst_ref=low_got.at[t],
            send_sem=part_send.at[m],
            recv_sem=part_recv.at[t],
            device_id={"tensor": owners[m]},
            device_id_type=MESH,
        )

    def part_arrival(d):
        source = lax.rem(t + n - d, n)
        return pltpu.make_async_remote_copy(
            src_ref=low_got.at[source],
            dst_ref=low_got.at[source],
            send_sem=part_send.at[0],
            recv_sem=part_recv.at[source],
            device_id={"tensor": source},
            device_id_type=MESH,
        )

    def low_copy(d):
        held = low_all.at[pair_rows(own_pair), :]
        return pltpu.make_async_remote_copy(
            src_ref=held,
            dst_ref=held,
            send_sem=low_send.at[d],
            recv_sem=low_recv.at[own_pair],
            device_id={"tensor": lax.rem(t + d, n)},
            device_id_type=MESH,
        )

    def low_arrival(m):
        held = low_all.at[pair_rows(m), :]
        return pltpu.make_async_remote_copy(
            src_ref=held,
            dst_ref=held,
            send_sem=low_send.at[0],
            recv_sem=low_recv.at[m],
            device_id={"tensor": owners[m]},
            device_id_type=MESH,
        )

    def adapters_arrive():
        for d in range(1, stores):
            source = lax.rem(s + stores - d, stores)
            for i, (_, held) in enumerate(adapter_pairs):
                block = adapter_block(held, i, source)
                pltpu.make_async_remote_copy(
                    src_ref=block,
                    dst_ref=block,
                    send_sem=adapter_send.at[i, d],
                    recv_sem=adapter_recv.at[i, d],
                    device_id={"store": source},
                    device_id_type=MESH,
                ).wait_recv()

    def low_first():
        fill_holder()
        adapters_arrive()
        summed = jnp.zeros(low_part.shape, jnp.float32)
        for p in range(stores):
            picked = jnp.zeros(low_part.shape, jnp.float32)
            for k in range(share):
                picked += lax.dot_general(
                    xbuf[t * share + k],
                    down[p, :, k * width : (k + 1) * width],
                    (((1,), (1,)), ((), ())),
                    preferred_element_type=jnp.float32,
                )
            summed += picked * mask_of(p)
        low_part[...] = summed.astype(jnp.bfloat16)
        low_own[...] = summed
        for m in range(pairs):

            @pl.when(t != owners[m])
            def _():
                part_copy(m).start()

    def low_second():
        at = pair_rows(own_pair)
        whole = low_own[at, :]
        for d in range(1, n):
            part_arrival(d).wait_recv()
            whole += low_got[lax.rem(t + n - d, n)].astype(jnp.float32)
        low_all[at, :] = whole.astype(jnp.bfloat16)
        for d in range(1, n):
            low_copy(d).start()

    def spread_low(lower):
        low = low_all[...].astype(jnp.float32)
        turned = pltpu.roll(low, ADAPTER_RANK, 1)
        in_lower = lax.broadcasted_iota(jnp.int32, low.shape, 1) < ADAPTER_RANK
        twice = jnp.where(in_lower, low, turned) if lower else jnp.where(in_lower, turned, low)
        masks = [
            jnp.where(in_lower, mask_of(2 * p), mask_of(2 * p + 1)) for p in range(stores // 2)
        ]
        return jnp.concatenate([(twice * m).astype(jnp.bfloat16) for m in masks], axis=1)

    def low_keyval():
        for m in range(pairs):

            @pl.when(t != owners[m])
            def _():
                low_arrival(m).wait_recv()

        acc_kv[...] += adapter_scale * jnp.dot(
            spread_low(False), upkv[...], preferred_element_type=jnp.float32
        )

    def low_query():
        spread = spread_low(True)
        for k in range(query_width // tile_q):
            columns = slice(k * tile_q, (k + 1) * tile_q)
            acc_q[:, columns] += adapter_scale * jnp.dot(
                spread, upq[:, columns], preferred_element_type=jnp.float32
            )

    def rotated(value, cosine, sine):
        return value * cosine + pltpu.roll(value, HEAD_SIZE // 2, 1) * sine

    ends_first = t >= n - t
    early_start = pl.multiple_of(jnp.where(ends_first, rows, 0), rows)
    late_start = pl.multiple_of(jnp.where(ends_first, 0, total - rows), rows)
    partner = t + 1 - 2 * (t % 2)

    def finish_keyval(start, count):
        at = pl.ds(start, count)
        cosine = jnp.where(holds_keys, cos_ref[at, :], 1.0)
        sine = jnp.where(holds_keys, sin_ref[at, :], 0.0)
        for m in range(pair_heads):
            value = acc_kv[at, m * HEAD_SIZE : (m + 1) * HEAD_SIZE]
            kv_heads[m, at, :] = rotated(value, cosine, sine).astype(jnp.bfloat16)

    def keyval_copy(start, count, which):
        at = pl.ds(start, count)
        return pltpu.make_async_remote_copy(
            src_ref=kv_heads.at[pl.ds(kv_first(partner), kv_used), at, :],
            dst_ref=kv_got.at[:, at, :],
            send_sem=kv_sem.at[0, which],
            recv_sem=kv_sem.at[1, which],
            device_id={"tensor": partner},
            device_id_type=MESH,
        )

    own_first = kv_first(t)
    is_inner = jnp.logical_not(is_end)
    starts_first = jnp.logical_not(ends_first)
    holds_values = jnp.logical_not(holds_keys)
    early_count = total - rows
    per_kv = head_local // kv_used
    batch = min(8, per_kv)
    block = 128
    blocks = total // block
    scale = 1.0 / math.sqrt(HEAD_SIZE) / math.log(2.0)
    stage_at = pl.multiple_of(jnp.where(ends_first, model_width - total, 0), total)
    part_at = pl.multiple_of(jnp.where(ends_first, model_width - 2 * total, total), total)

    def finish_late():
        finish_keyval(late_start, rows)
        keyval_copy(late_start, rows, 1).start()

    def gather_keys(start, count):
        at = pl.ds(start, count)
        for g in range(kv_used):

            @pl.when(holds_keys)
            def _():
                keys_ref[g, at, :] = kv_heads[own_first + g, at, :]

            @pl.when(holds_values)
            def _():
                keys_ref[g, at, :] = kv_got[g, at, :]

    def gather_values(start, count):
        at = pl.ds(start, count)
        for g in range(kv_used):

            @pl.when(holds_keys)
            def _():
                values_ref[g, at, :HEAD_SIZE] = kv_got[g, at, :]

            @pl.when(holds_values)
            def _():
                values_ref[g, at, :HEAD_SIZE] = kv_heads[own_first + g, at, :]

    def lanes_of(h):
        return pl.ds(pl.multiple_of(h * HEAD_SIZE, HEAD_SIZE), HEAD_SIZE)

    def stage_rows(start, first, count):
        return pl.ds(pl.multiple_of(start + first, block), count)

    def scores_of(b, g, lanes, low, high):
        at = slice(b * block, (b + 1) * block)
        query = [
            rotated(acc_q[at, ln], cos_ref[at, :], sin_ref[at, :]).astype(jnp.bfloat16)
            for ln in lanes
        ]
        scores = lax.dot_general(
            jnp.concatenate(query, axis=0),
            keys_ref[g, low:high, :],
            (((1,), (1,)), ((), ())),
            preferred_element_type=jnp.float32,
        )
        scores = scores.reshape(2, block, high - low) + bias_ref[at, low:high][None]
        return scores.reshape(2 * block, high - low)

    def weights_of(b, g, lanes):
        scores = scores_of(b, g, lanes, max(0, b * block - MAX_RUN), (b + 1) * block)
        scores = (scores - jnp.max(scores, axis=1, keepdims=True)) * scale
        return jnp.exp2(scores).astype(jnp.bfloat16)

    def attend(b, g, lanes):
        low = max(0, b * block - MAX_RUN)
        high = (b + 1) * block
        mixed = jnp.dot(
            weights_of(b, g, lanes), values_ref[g, low:high, :], preferred_element_type=jnp.float32
        )
        mixed = (mixed[:, :HEAD_SIZE] / mixed[:, HEAD_SIZE:]).astype(jnp.bfloat16)
        for k, ln in enumerate(lanes):
            wq[stage_rows(stage_at, b * block, block), ln] = mixed[k * block : (k + 1) * block]

    def attend_part(b, g, lanes):
        high = (b + 1) * block
        weights = weights_of(b, g, lanes)
        first = weights[:, :block]
        sums = jnp.dot(
            first, values_ref[g, :block, HEAD_SIZE:], preferred_element_type=jnp.float32
        )
        if b > 0:
            mixed = jnp.dot(
                weights[:, block:], values_ref[g, block:high, :], preferred_element_type=jnp.float32
            )
            sums += mixed[:, HEAD_SIZE:]
        inverse = 1.0 / sums
        rest = mixed[:, :HEAD_SIZE] * inverse if b > 0 else jnp.zeros_like(inverse)
        first = (first.astype(jnp.float32) * inverse).astype(jnp.bfloat16)
        for k, ln in enumerate(lanes):
            acc_q[b * block : high, ln] = rest[k * block : (k + 1) * block]
            wq[stage_rows(part_at, b * block, block), ln] = first[k * block : (k + 1) * block]

    def attend_rest(b, g, lanes):
        ln = pl.ds(lanes[0].start, 2 * HEAD_SIZE)
        first, count = b * block, (blocks - 1 - b) * block
        more = jnp.dot(
            wq[stage_rows(part_at, first, count), ln],
            twin_ref[g],
            preferred_element_type=jnp.float32,
        )
        whole = acc_q[first : first + count, ln] + more
        wq[stage_rows(stage_at, first, count), ln] = whole.astype(jnp.bfloat16)

    last = (blocks - 1) * block
    kept = [slice(k * block, (k + 1) * block) for k in range(3)]

    def attend_start(g, lanes):
        scores = scores_of(blocks - 1, g, lanes, last - MAX_RUN, last)
        top = jnp.max(scores, axis=1, keepdims=True)
        weights = jnp.exp2((scores - top) * scale).astype(jnp.bfloat16)
        mixed = jnp.dot(
            weights, values_ref[g, last - MAX_RUN : last, :], preferred_element_type=jnp.float32
        )
        for k, ln in enumerate(lanes):
            at = slice(k * block, (k + 1) * block)
            acc_q[kept[0], ln] = mixed[at, :HEAD_SIZE]
            acc_q[kept[1], ln] = mixed[at, HEAD_SIZE:]
            acc_q[kept[2], ln] = jnp.broadcast_to(top[at], (block, HEAD_SIZE))

    def attend_finish(g, lanes):
        at = slice(last, total)
        query = [
            rotated(acc_q[at, ln], cos_ref[at, :], sin_ref[at, :]).astype(jnp.bfloat16)
            for ln in lanes
        ]
        both = lax.dot_general(
            jnp.concatenate(query, axis=1),
            twin_keys_ref[g],
            (((1,), (1,)), ((), ())),
            preferred_element_type=jnp.float32,
        )
        weights, shrinks, sums = [], [], []
        for k, ln in enumerate(lanes):
            scores = both[:, k * block : (k + 1) * block] + bias_ref[at, last:total]
            top_of = acc_q[kept[2], ln]
            top = jnp.maximum(top_of, jnp.max(scores, axis=1, keepdims=True))
            weights.append(jnp.exp2((scores - top) * scale).astype(jnp.bfloat16))
            shrinks.append(jnp.exp2((top_of - top) * scale))
            more = jnp.sum(weights[k].astype(jnp.float32), axis=1, keepdims=True)
            sums.append(acc_q[kept[1], ln] * shrinks[k] + more)
        mixed = jnp.dot(
            jnp.concatenate(weights, axis=1), twin_ref[g], preferred_element_type=jnp.float32
        )
        for k, ln in enumerate(lanes):
            whole = acc_q[kept[0], ln] * shrinks[k] + mixed[:, k * block : (k + 1) * block]
            wq[stage_rows(stage_at, last, block), ln] = (whole / sums[k]).astype(jnp.bfloat16)

    cut = total - block

    def out_copy(q, which):
        first, count = (0, cut) if which == 0 else (cut, block)
        lanes = pl.ds(pl.multiple_of(q * batch * HEAD_SIZE, batch * HEAD_SIZE), batch * HEAD_SIZE)
        return pltpu.make_async_copy(
            wq.at[stage_rows(stage_at, first, count), lanes],
            out_ref.at[pl.ds(first, count), lanes],
            out_sem.at[which, q],
        )

    def heads(body, which, q):
        g = q * batch // per_kv
        for pair in range(batch // 2):
            body(g, [lanes_of(q * batch + 2 * pair + k) for k in range(2)])
        out_copy(q, which).start()

    def over_heads(body, which):
        @pl.loop(0, head_local // batch)
        def _(q):
            heads(body, which, q)

    def early_keyval():
        keyval_copy(early_start, early_count, 0).wait_recv()
        gather_keys(early_start, early_count)
        gather_values(early_start, early_count)

        @pl.when(ends_first)
        def _():
            @pl.when(holds_values)
            def _():
                keyval_copy(late_start, rows, 1).wait_recv()

            gather_keys(late_start, rows)

    def early_attention(q):
        def lower(inner):
            def body(g, lanes):
                for b in range(blocks - 1):
                    attend(b, g, lanes)
                if inner:
                    attend_start(g, lanes)

            return body

        def upper(inner):
            def body(g, lanes):
                attend(blocks - 1, g, lanes)
                for b in range(0 if inner else 1, blocks - 1):
                    attend_part(b, g, lanes)

            return body

        for inner, where in ((False, is_end), (True, is_inner)):

            @pl.when(jnp.logical_and(where, starts_first))
            def _():
                heads(lower(inner), 0, q)

            @pl.when(jnp.logical_and(where, ends_first))
            def _():
                heads(upper(inner), 1, q)

    def late_attention():
        def lower(inner):
            def body(g, lanes):
                if inner:
                    attend_finish(g, lanes)
                else:
                    attend(blocks - 1, g, lanes)

            return body

        def upper(inner):
            def body(g, lanes):
                if not inner:
                    attend(0, g, lanes)
                attend_rest(0 if inner else 1, g, lanes)

            return body

        @pl.when(starts_first)
        def _():
            keyval_copy(late_start, rows, 1).wait_recv()
            gather_keys(late_start, rows)
            gather_values(late_start, rows)
            for g in range(kv_used):
                for k in range(2):
                    at = slice(k * block, (k + 1) * block)
                    twin_ref[g, at, at] = values_ref[g, last:total, :HEAD_SIZE]
                    twin_keys_ref[g, at, at] = keys_ref[g, last:total, :]

        @pl.when(ends_first)
        def _():
            @pl.when(holds_keys)
            def _():
                keyval_copy(late_start, rows, 1).wait_recv()

            gather_values(late_start, rows)
            for g in range(kv_used):
                value = values_ref[g, :block, :HEAD_SIZE]
                twin_ref[g, :block, :HEAD_SIZE] = value
                twin_ref[g, block:, HEAD_SIZE:] = value

        for inner, where in ((False, is_end), (True, is_inner)):

            @pl.when(jnp.logical_and(where, starts_first))
            def _():
                over_heads(lower(inner), 1)

            @pl.when(jnp.logical_and(where, ends_first))
            def _():
                over_heads(upper(inner), 0)

    twin_ref[...] = jnp.zeros_like(twin_ref)
    twin_keys_ref[...] = jnp.zeros_like(twin_keys_ref)
    for g in range(kv_used):
        values_ref[g, :, HEAD_SIZE:] = jnp.ones((total, HEAD_SIZE), jnp.bfloat16)

    @pl.loop(0, last_step)
    def _(step):
        here = tuple(step < reach[side] * chunks for side in range(2))
        places = [item(reach[side], step) for side in range(2)]
        for side in range(2):
            p, i = places[side]

            @pl.when(here[side])
            def _():
                arrival(side, p, i).wait_recv()

            sends = (reach[side] + 1) * chunks
            head = (reach[side] + 1) * share

            @pl.when(jnp.logical_and(can_send[side], step + depth - 1 < sends))
            def _():
                send_item(side, step, False).wait_send()

                @pl.when(step + ahead <= head)
                def _():
                    start_send(side, step + ahead)

                @pl.when(step + ahead == head)
                def _():
                    for j in range(1, depth - 1):
                        start_send(side, step + ahead + j)

                nearer = step > inner_done
                later = step + depth - jnp.where(nearer, 1, 0)
                wanted = jnp.logical_and(step + ahead > head, step != inner_done + 1)

                @pl.when(jnp.logical_and(wanted, later < sends))
                def _():
                    start_send(side, later)

        @pl.when(step < chunks // 2)
        def _():
            for c in (step, chunks - 1 - step):
                for copy in weight_copies(c):
                    copy.wait()

            @pl.when(step + 1 < chunks // 2)
            def _():
                start_weights(step + 1)

        for side in range(2):
            p, i = places[side]

            @pl.when(here[side])
            def _():
                keyval_unit(place(side, i), t - p if side == 0 else t + p)

        for side in range(2):
            p, i = places[side]

            @pl.when(here[side])
            def _():
                query_unit(place(side, i), t - p if side == 0 else t + p)

        @pl.when(jnp.logical_and(step >= chunks, step < 2 * chunks))
        def _():
            keyval_unit(step - chunks, t)
            query_unit(step - chunks, t)

        @pl.when(step == chunks - 2)
        def _():
            fill_tables()

        @pl.when(step == low_at)
        def _():
            low_first()

        @pl.when(jnp.logical_and(is_owner, step == inner_done))
        def _():
            low_second()

        @pl.when(step == third_at)
        def _():
            low_keyval()
            finish_keyval(early_start, early_count)
            keyval_copy(early_start, early_count, 0).start()

            @pl.when(is_inner)
            def _():
                finish_late()

            low_query()

        @pl.when(step == early_at)
        def _():
            early_keyval()

        @pl.when(jnp.logical_and(step >= early_at, step < early_at + head_local // batch))
        def _():
            early_attention(step - early_at)

    @pl.when(is_end)
    def _():
        at = pl.ds(late_start, rows)
        for h in range(2):
            half_copy(h).wait_recv()
            part = pl.ds(pl.multiple_of(last_chunk * width + h * half, half), half)
            x = xbuf[last_chunk, at, h * half : (h + 1) * half]
            acc_kv[at, :] += jnp.dot(x, wkv[part, :], preferred_element_type=jnp.float32)
            if h == 1:
                finish_late()

            @pl.loop(0, query_width // tile_q)
            def _(k):
                columns = pl.ds(pl.multiple_of(k * tile_q, tile_q), tile_q)
                acc_q[at, columns] += jnp.dot(
                    xbuf[last_chunk, at, h * half : (h + 1) * half],
                    wq[part, columns],
                    preferred_element_type=jnp.float32,
                )

    late_attention()

    for copy in adapter_sends:
        copy.wait_send()
    for m in range(pairs):

        @pl.when(t != owners[m])
        def _():
            part_copy(m).wait_send()

    @pl.when(is_owner)
    def _():
        for d in range(1, n):
            low_copy(d).wait_send()

    keyval_copy(early_start, early_count, 0).wait_send()
    keyval_copy(late_start, rows, 1).wait_send()

    for side in range(2):

        @pl.when(can_send[side])
        def _():
            for j in range(1, depth - 1):
                send_item(side, (reach[side] + 1) * chunks - depth + j, False).wait_send()

            @pl.when(reach[side] < n - 2)
            def _():
                send_item(side, (reach[side] + 1) * chunks - 1, False).wait_send()

            @pl.when(reach[side] == n - 2)
            def _():
                for h in range(2):
                    half_copy(h).wait_send()

    @pl.loop(0, head_local // batch)
    def _(q):
        for which in range(2):
            out_copy(q, which).wait()


def on_device(
    tokens,
    query_weight,
    key_value_weight,
    adapter_down_maps,
    adapter_up_query,
    adapter_up_key_value,
    adapter_row_table,
    request_adapter_ids,
    token_request_ids,
):
    n = lax.axis_size("tensor")
    stores = lax.axis_size("store")
    slots = adapter_down_maps.shape[0]
    rows, model_width = tokens.shape
    total = rows * n
    query_width = query_weight.shape[1]
    keyval_width = key_value_weight.shape[1]
    chunks = max(8, 2 * n)
    width = model_width // chunks
    pair_heads = keyval_width // HEAD_SIZE
    kv_used = max(query_width // HEAD_SIZE // (QUERY_HEADS // KEY_VALUE_HEADS), 1)
    two_ranks = 2 * ADAPTER_RANK
    hbm = pl.BlockSpec(memory_space=pl.ANY)
    vmem = pl.BlockSpec(memory_space=pltpu.VMEM)
    smem = pl.BlockSpec(memory_space=pltpu.SMEM)
    dma = pltpu.SemaphoreType.DMA
    results = pl.pallas_call(
        functools.partial(project_kernel, n, stores, chunks, slots),
        in_specs=[hbm] * 6 + [smem, smem, vmem],
        out_specs=[hbm] * 4,
        out_shape=[
            jax.ShapeDtypeStruct((total, query_width), jnp.bfloat16),
            jax.ShapeDtypeStruct((stores, two_ranks, query_width), jnp.bfloat16),
            jax.ShapeDtypeStruct((stores, ADAPTER_RANK, query_width), jnp.bfloat16),
            jax.ShapeDtypeStruct((stores, ADAPTER_RANK, keyval_width), jnp.bfloat16),
        ],
        scratch_shapes=[
            pltpu.VMEM((chunks, total, width), jnp.bfloat16),
            pltpu.VMEM((model_width, query_width), jnp.bfloat16),
            pltpu.VMEM((model_width, keyval_width), jnp.bfloat16),
            pltpu.VMEM((total, query_width), jnp.float32),
            pltpu.VMEM((total, keyval_width), jnp.float32),
            pltpu.VMEM((stores, two_ranks, model_width // n), jnp.bfloat16),
            pltpu.VMEM((stores * ADAPTER_RANK, query_width), jnp.bfloat16),
            pltpu.VMEM((stores * ADAPTER_RANK, keyval_width), jnp.bfloat16),
            pltpu.VMEM((total, two_ranks), jnp.bfloat16),
            pltpu.VMEM((total, two_ranks), jnp.float32),
            pltpu.VMEM((n, 2 * rows, two_ranks), jnp.bfloat16),
            pltpu.VMEM((total, two_ranks), jnp.bfloat16),
            pltpu.VMEM((pair_heads, total, HEAD_SIZE), jnp.bfloat16),
            pltpu.VMEM((kv_used, total, HEAD_SIZE), jnp.bfloat16),
            pltpu.VMEM((kv_used, total, HEAD_SIZE), jnp.bfloat16),
            pltpu.VMEM((kv_used, total, 2 * HEAD_SIZE), jnp.bfloat16),
            pltpu.VMEM((kv_used, 2 * HEAD_SIZE, 2 * HEAD_SIZE), jnp.bfloat16),
            pltpu.VMEM((kv_used, 2 * HEAD_SIZE, 2 * HEAD_SIZE), jnp.bfloat16),
            pltpu.VMEM((total, total), jnp.float32),
            pltpu.VMEM((total, HEAD_SIZE), jnp.float32),
            pltpu.VMEM((total, HEAD_SIZE), jnp.float32),
            pltpu.VMEM((total, 1), jnp.float32),
            dma((chunks,)),
            dma((2, chunks)),
            dma((2, n, chunks)),
            dma((2, n, chunks)),
            dma((3, stores)),
            dma((3, stores)),
            dma((3,)),
            dma((3, slots)),
            dma((3, stores)),
            dma((n,)),
            dma((n,)),
            dma((n,)),
            dma((n,)),
            dma((2, 2)),
            dma((2, 2)),
            dma((2, query_width // HEAD_SIZE)),
        ],
        compiler_params=pltpu.CompilerParams(
            collective_id=0, has_side_effects=True, vmem_limit_bytes=67043328
        ),
        name="project",
    )(
        tokens,
        query_weight,
        key_value_weight,
        adapter_down_maps,
        adapter_up_query,
        adapter_up_key_value,
        adapter_row_table,
        request_adapter_ids,
        token_request_ids,
    )
    return hand_over(results[0])


def hand_over_kernel(pieces, source, out, held, in_sem, out_sem):
    count = held.shape[0] // pieces

    def load(k):
        at = pl.ds(k * count, count)
        return pltpu.make_async_copy(source.at[at, :], held.at[at, :], in_sem.at[k])

    def store(k):
        at = pl.ds(k * count, count)
        return pltpu.make_async_copy(held.at[at, :], out.at[at, :], out_sem.at[k])

    for k in range(pieces):
        load(k).start()
    for k in range(pieces):
        load(k).wait()
        store(k).start()
    for k in range(pieces):
        store(k).wait()


def hand_over(attention):
    hbm = pl.BlockSpec(memory_space=pl.ANY)
    pieces = 8
    return pl.pallas_call(
        functools.partial(hand_over_kernel, pieces),
        in_specs=[hbm],
        out_specs=hbm,
        out_shape=jax.ShapeDtypeStruct(attention.shape, attention.dtype),
        scratch_shapes=[
            pltpu.VMEM(attention.shape, attention.dtype),
            pltpu.SemaphoreType.DMA((pieces,)),
            pltpu.SemaphoreType.DMA((pieces,)),
        ],
        name="hand_over",
    )(attention)


def solution(mesh):
    return jax.shard_map(
        on_device,
        mesh=mesh,
        in_specs=(
            P(("groups", "store", "tensor"), None),
            P(None, "tensor"),
            P(None, "tensor"),
            P("store", None, "tensor"),
            P("store", None, "tensor"),
            P("store", None, "tensor"),
            P("groups"),
            P("groups", None),
            P(("groups", "store"), None),
        ),
        out_specs=P(("groups", "store"), "tensor"),
        check_vma=False,
    )
```
